32 devices in a mesh: fsdp: 8 (over z, y), ctx: 2 (over x), tp: 2 (over core).
Axes of the slice: x: 2, y: 2, z: 4, core: 2. Of those that a mesh axis runs over, the one named last changes fastest.
Arguments:
- tokens_in: bfloat16 [4096, 2048], P(('fsdp', 'ctx')), may hold values from -6 to 6
- doc_positions: int32 [4096], P(('fsdp', 'ctx')), may hold values from 0 to 383, as said below
- attn_gain: bfloat16 [2048], P('fsdp'), may hold values from 0.25 to 1.75
- query_weight: bfloat16 [2048, 2048], P('fsdp', 'tp'), may hold values from -1 to 1
- key_weight: bfloat16 [2048, 256], P('fsdp', 'tp'), may hold values from -1 to 1
- value_weight: bfloat16 [2048, 256], P('fsdp', 'tp'), may hold values from -0.125 to 0.125
- output_weight: bfloat16 [2048, 2048], P('fsdp', 'tp'), may hold values from -2 to 2
- mlp_gain: bfloat16 [2048], P('fsdp'), may hold values from 0.25 to 1.75
- gate_weight: bfloat16 [2048, 5632], P('fsdp', 'tp'), may hold values from -0.125 to 0.125
- up_weight: bfloat16 [2048, 5632], P('fsdp', 'tp'), may hold values from -0.125 to 0.125
- down_weight: bfloat16 [2048, 5632], P('fsdp', 'tp'), may hold values from -0.078125 to 0.078125
- cotangent: bfloat16 [4096, 2048], P(('fsdp', 'ctx')), may hold values from -6 to 6
Outputs:
- block_out: bfloat16 [4096, 2048], P(('fsdp', 'ctx'))
- grad_tokens: float32 [4096, 2048], P(('fsdp', 'ctx'))
- grad_attn_gain: float32 [2048], P('fsdp')
- grad_query: float32 [2048, 2048], P('fsdp', 'tp')
- grad_key: float32 [2048, 256], P('fsdp', 'tp')
- grad_value: float32 [2048, 256], P('fsdp', 'tp')
- grad_output: float32 [2048, 2048], P('fsdp', 'tp')
- grad_mlp_gain: float32 [2048], P('fsdp')
- grad_gate: float32 [2048, 5632], P('fsdp', 'tp')
- grad_up: float32 [2048, 5632], P('fsdp', 'tp')
- grad_down: float32 [2048, 5632], P('fsdp', 'tp')
The draws below stay inside these ranges and needn't reach their ends.
Inputs may be any that keep to these rules, and one draw needn't show every extreme that they name: `doc_positions`: each sequence of 512 tokens is packed with documents and begins with a new one; a token's value is its offset within its document: 0 at a document's first token, rising by one along it. Documents hold 102 to 384 tokens, except that the last of a sequence may be cut short; some document holds exactly 384.
All inputs are finite; a program needn't handle non-finite values.
Results may differ from the reference program's by a relative error of at most 0.014.
The reference program's roundings to bfloat16 on the way count: a program that leaves them out, or rounds other values in their place, can miss the bound.
Values may be sent and summed in bfloat16 or wider, within the bound.
No kernel may reach another device: no remote copies, remote signals or barrier semaphores. Data moves between devices by JAX's collectives and lax.ppermute only.
A program may use at most 256 MiB of HBM per device.

```python
import jax
import jax.numpy as jnp
from jax import lax

D = 2048
HEADS = 32
KV_HEADS = 4
HEAD_DIM = 64
FF = 5632
LEN = 512
TOKENS = 4096
DOC_MIN = 102
DOC_MAX = 384


def draw_doc_positions(key, part):
    seq_count = TOKENS // LEN
    slots = LEN // DOC_MIN + 1
    lengths = jax.random.randint(jax.random.fold_in(key, 101), (seq_count, slots), DOC_MIN, DOC_MAX + 1)
    chosen = jax.random.randint(jax.random.fold_in(key, 102), (), 0, seq_count)
    forced = (jnp.arange(seq_count)[:, None] == chosen) & (jnp.arange(slots)[None, :] == 0)
    lengths = jnp.where(forced, DOC_MAX, lengths)
    starts = jnp.cumsum(lengths, axis=1) - lengths
    places = jnp.arange(LEN)
    begun = jnp.where(starts[:, None, :] <= places[None, :, None], starts[:, None, :], 0)
    latest = jnp.max(begun, axis=2)
    return (places[None, :] - latest).reshape(-1).astype(jnp.int32)


def shared_heads(key):
    base = jax.random.truncated_normal(jax.random.fold_in(key, 201), -4.0, 4.0, (D, HEADS * HEAD_DIM), jnp.float32) * D ** (-0.5)
    return base


def draw_query_weight(key, part):
    base = shared_heads(key)
    return jnp.clip(base, -1.0, 1.0).astype(jnp.bfloat16)


def draw_key_weight(key, part):
    return jnp.clip(jax.random.truncated_normal(jax.random.fold_in(key, 203), -4.0, 4.0, (D, KV_HEADS * HEAD_DIM), jnp.float32) * D ** (-0.5), -1.0, 1.0).astype(jnp.bfloat16)


def with_spikes(array, key, source, target, parts, factor):
    owner, partner = [(jnp.arange(array.shape[axis_at]) // (array.shape[axis_at] // parts)).reshape([-1 if axis == axis_at else 1 for axis in range(array.ndim)]) for axis_at in (source, target)]
    chosen = jax.random.permutation(key, parts)[partner]
    strong = (owner == chosen) | (owner == (partner + parts // 2) % parts)
    return jnp.where(strong, factor * array, array)


def block_scale(rng, dims, split, smallest, high):
    gain = 1.0
    for dim, shards_of in split:
        steps = jax.random.uniform(jax.random.fold_in(jax.random.fold_in(rng, 6), dim), (shards_of,), jnp.float32, smallest / len(split), high / len(split))
        gain = gain * jnp.repeat(jnp.exp(steps), dims[dim] // shards_of).reshape((-1,) + (1,) * (len(dims) - 1 - dim))
    return gain


def noise(key, dims, scale, reach, split=(), kind=jnp.bfloat16):
    loudness = block_scale(key, dims, split, -0.22, 0.18) if split else 1.0
    values = jax.random.normal(key, dims, jnp.float32) * scale * loudness
    return jnp.minimum(jnp.maximum(values, -reach), reach).astype(kind)


def gaussian_with(stream_key, dims, width, bound, split, heavy, kind=jnp.bfloat16):
    values = width * jax.random.normal(stream_key, dims, jnp.float32)
    if split:
        values = values * block_scale(stream_key, dims, split, -0.22, 0.18)
    return jnp.clip(with_spikes(values, jax.random.fold_in(stream_key, 3), *heavy), -bound, bound).astype(kind)


def setup_inputs(seed: int = 0) -> dict:
    streams_of = jax.random.split(jax.random.key(seed), 13)
    return {
        "tokens_in": noise(streams_of[0], (TOKENS, D), 1.0, 6.0, ((0, 16),)),
        "doc_positions": draw_doc_positions(jax.random.fold_in(streams_of[12], 71), 0),
        "attn_gain": jnp.clip(1.0 + 0.15 * jax.random.normal(streams_of[2], (D,), jnp.float32), 0.25, 1.75).astype(jnp.bfloat16),
        "query_weight": draw_query_weight(jax.random.fold_in(streams_of[12], 71), 0),
        "key_weight": draw_key_weight(jax.random.fold_in(streams_of[12], 71), 0),
        "value_weight": noise(streams_of[5], (D, KV_HEADS * HEAD_DIM), D ** -0.5, 0.125, ((0, 8), (1, 2))),
        "output_weight": noise(streams_of[6], (D, HEADS * HEAD_DIM), (max(HEADS * HEAD_DIM // 256, 4)) ** -0.5, 2.0, ((0, 8), (1, 2))),
        "mlp_gain": jnp.clip(1.0 + 0.15 * jax.random.normal(streams_of[7], (D,), jnp.float32), 0.25, 1.75).astype(jnp.bfloat16),
        "gate_weight": noise(streams_of[8], (D, FF), D ** -0.5, 0.125, ((0, 8), (1, 2))),
        "up_weight": noise(streams_of[9], (D, FF), D ** -0.5, 0.125, ((0, 8), (1, 2))),
        "down_weight": noise(streams_of[10], (D, FF), FF ** -0.5, 0.078125, ((0, 8), (1, 2))),
        "cotangent": gaussian_with(streams_of[11], (TOKENS, D), 1.0, 6.0, ((0, 16),), (0, 1, 16, 2.0)),
    }


EPSILON = 1e-05
NEG_FILL = -1e+30

@jax.custom_vjp
def low(v):
    return lax.optimization_barrier(v.astype(jnp.bfloat16)).astype(jnp.float32)

@jax.custom_vjp
def low_back(v):
    return v

def low_keep(v):
    return (low(v), None)

def low_pass(kept, grad):
    return (grad,)

def back_keep(v):
    return (v, None)

def back_low(kept, grad):
    return (low(grad),)
low.defvjp(low_keep, low_pass)
low_back.defvjp(back_keep, back_low)

def rotary_tables(positions):
    half_dim = HEAD_DIM // 2
    inverse = 1.0 / 10000.0 ** (jnp.arange(half_dim, dtype=jnp.float32) * (2.0 / HEAD_DIM))
    angles = positions.astype(jnp.float32)[:, None] * inverse[None, :]
    cosine_table = jnp.concatenate([jnp.cos(angles), jnp.cos(angles)], axis=-1)[:, None, :]
    sine_table = jnp.concatenate([jnp.sin(angles), jnp.sin(angles)], axis=-1)[:, None, :]
    return (cosine_table, sine_table)

def apply_rotary(values, cosine_table, sine_table):
    half_dim = values.shape[-1] // 2
    turned = jnp.concatenate([-values[..., half_dim:], values[..., :half_dim]], axis=-1)
    return values * cosine_table + turned * sine_table

def matmul_high(left_array, right_array):
    return jnp.dot(left_array, right_array, precision=lax.Precision.HIGHEST)

def attend_sequence(pieces):
    queries, key_rows, value_rows, positions = pieces
    group_size = HEADS // KV_HEADS
    places = jnp.arange(LEN, dtype=jnp.int32)
    starts = places - positions.astype(jnp.int32)
    allowed = (places[None, :] <= places[:, None]) & (places[None, :] >= starts[:, None])
    grouped = queries.reshape(LEN, KV_HEADS, group_size, HEAD_DIM)
    key_heads = key_rows.reshape(LEN, KV_HEADS, HEAD_DIM)
    value_heads = value_rows.reshape(LEN, KV_HEADS, HEAD_DIM)
    scores = jnp.einsum('nhgd,khd->hgnk', grouped, key_heads, precision=lax.Precision.HIGHEST)
    scores = low_back(scores * HEAD_DIM ** (-0.5))
    scores = jnp.where(allowed[None, None], scores, NEG_FILL)
    largest = lax.optimization_barrier(jnp.max(scores, axis=-1, keepdims=True))
    exponent = jnp.exp(scores - largest)
    probabilities = low(exponent / lax.optimization_barrier(jnp.sum(exponent, axis=-1, keepdims=True)))
    attended = jnp.einsum('hgnk,khd->nhgd', probabilities, value_heads, precision=lax.Precision.HIGHEST)
    return attended.reshape(LEN, HEADS * HEAD_DIM)

def reference(tokens_in, doc_positions, attn_gain, query_weight, key_weight, value_weight, output_weight, mlp_gain, gate_weight, up_weight, down_weight, cotangent):
    cosine_table, sine_table = rotary_tables(doc_positions)
    seq_count = TOKENS // LEN

    def forward(tokens, gain_one, query_matrix, key_matrix, value_matrix, output_matrix, gain_two, gate_matrix, up_matrix, down_matrix):
        rms_one = lax.rsqrt(lax.optimization_barrier(jnp.mean(tokens * tokens, axis=-1, keepdims=True)) + EPSILON)
        normed_one = low(tokens * rms_one * gain_one)
        query_lin = low_back(matmul_high(normed_one, query_matrix)).reshape(TOKENS, HEADS, HEAD_DIM)
        key_lin = low_back(matmul_high(normed_one, key_matrix)).reshape(TOKENS, KV_HEADS, HEAD_DIM)
        queries = low(apply_rotary(query_lin, cosine_table, sine_table)).reshape(seq_count, LEN, HEADS * HEAD_DIM)
        key_rows = low(apply_rotary(key_lin, cosine_table, sine_table)).reshape(seq_count, LEN, KV_HEADS * HEAD_DIM)
        value_rows = low(low_back(matmul_high(normed_one, value_matrix))).reshape(seq_count, LEN, KV_HEADS * HEAD_DIM)
        attended = lax.map(jax.checkpoint(attend_sequence), (queries, key_rows, value_rows, doc_positions.reshape(seq_count, LEN)))
        attended = low(low_back(attended.reshape(TOKENS, HEADS * HEAD_DIM)))
        residual = tokens + low_back(matmul_high(attended, output_matrix.T))
        rms_two = lax.rsqrt(lax.optimization_barrier(jnp.mean(residual * residual, axis=-1, keepdims=True)) + EPSILON)
        normed_two = low(residual * rms_two * gain_two)
        gate_lin = low_back(matmul_high(normed_two, gate_matrix))
        up_lin = low_back(matmul_high(normed_two, up_matrix))
        act_low = low(gate_lin / (1.0 + jnp.exp(-gate_lin)) * up_lin)
        return residual + low_back(matmul_high(act_low, down_matrix.T))
    block_out, pull_back = jax.vjp(forward, tokens_in.astype(jnp.float32), attn_gain.astype(jnp.float32), query_weight.astype(jnp.float32), key_weight.astype(jnp.float32), value_weight.astype(jnp.float32), output_weight.astype(jnp.float32), mlp_gain.astype(jnp.float32), gate_weight.astype(jnp.float32), up_weight.astype(jnp.float32), down_weight.astype(jnp.float32))
    gradients = pull_back(cotangent.astype(jnp.float32))
    return (block_out.astype(jnp.bfloat16), gradients[0], gradients[1], gradients[2], gradients[3], gradients[4], gradients[5], gradients[6], gradients[7], gradients[8], gradients[9])
```

```python
import functools

import jax
import jax.numpy as jnp
from jax import lax
from jax.sharding import PartitionSpec as P

HEADS = 32
KV_HEADS = 4
HEAD_DIM = 64

EPSILON = 1e-05
NEG_FILL = -1e30


F32 = jnp.float32
BF16 = jnp.bfloat16


def rotary_tables(positions):
    half_dim = HEAD_DIM // 2
    inverse = 1.0 / 10000.0 ** (jnp.arange(half_dim, dtype=F32) * (2.0 / HEAD_DIM))
    angles = positions.astype(F32)[:, None] * inverse[None, :]
    cosine_table = jnp.concatenate([jnp.cos(angles), jnp.cos(angles)], axis=-1)[:, None, :]
    sine_table = jnp.concatenate([jnp.sin(angles), jnp.sin(angles)], axis=-1)[:, None, :]
    return (cosine_table, sine_table)


def apply_rotary(values, cosine_table, sine_table):
    half_dim = values.shape[-1] // 2
    turned = jnp.concatenate([-values[..., half_dim:], values[..., :half_dim]], axis=-1)
    return values * cosine_table + turned * sine_table


def undo_rotary(gradient, cosine_table, sine_table):
    half_dim = gradient.shape[-1] // 2
    sined = gradient * sine_table
    return gradient * cosine_table + jnp.concatenate(
        [sined[..., half_dim:], -sined[..., :half_dim]], axis=-1
    )


def dot_nt(left, right):
    return lax.dot_general(left, right, (((1,), (1,)), ((), ())), preferred_element_type=F32)


def dot_tn(left, right):
    return lax.dot_general(left, right, (((0,), (0,)), ((), ())), preferred_element_type=F32)


def dot_nn(left, right):
    return jnp.dot(left, right, preferred_element_type=F32)


class Plane:
    def __init__(self, size):
        self.size = size
        self.far = size // 2

    def swap(self, array, step):
        return lax.ppermute(array, "fsdp", [(i, i ^ step) for i in range(self.size)])

    def gather(self, shard):
        near = [shard] + [self.swap(shard, 2 * k) for k in range(1, self.far)]
        blocks = []
        for block in near:
            blocks += [block, self.swap(block, 1)]
        return blocks

    def exchange(self, blocks, low):
        here = low == 0
        kept = jnp.where(here, blocks[:, 0], blocks[:, 1])
        sent = jnp.where(here, blocks[:, 1], blocks[:, 0])
        got = self.swap(sent, 1)
        both = jnp.where(
            here, jnp.stack([kept, got], axis=1), jnp.stack([got, kept], axis=1)
        )
        return both

    def scatter_far(self, both, high):
        out = []
        for k in range(self.far):
            block = lax.dynamic_index_in_dim(both, high ^ k, 0, keepdims=False)
            out.append(block if k == 0 else self.swap(block, 2 * k))
        return out

    def all_to_all(self, blocks, high, low):
        return self.scatter_far(self.exchange(blocks, low), high)

    def reduce(self, blocks, wire=F32):
        odd = self.swap(jnp.stack([b.astype(wire) for b in blocks[1::2]]), 1)
        total = None
        for k in range(self.far):
            part = blocks[2 * k].astype(F32) + odd[k].astype(F32)
            if k:
                part = self.swap(part.astype(wire), 2 * k).astype(F32)
            total = part if total is None else total + part
        return total


def swap_pair(array, axis):
    return lax.ppermute(array, axis, [(0, 1), (1, 0)])


def place(blocks, index, size, axis):
    shape = list(blocks[0].shape)
    width = shape[axis]
    shape[axis] = width * size
    out = jnp.zeros(shape, blocks[0].dtype)
    for k, block in enumerate(blocks):
        out = lax.dynamic_update_slice_in_dim(out, block, (index ^ k) * width, axis)
    return out


def body(
    plane,
    tokens_in,
    doc_positions,
    attn_gain,
    query_weight,
    key_weight,
    value_weight,
    output_weight,
    mlp_gain,
    gate_weight,
    up_weight,
    down_weight,
    cotangent,
):
    nf = plane.size
    far = plane.far
    me = lax.axis_index("fsdp")
    high, low = me // 2, me % 2
    ctx = lax.axis_index("ctx")
    core = lax.axis_index("tp")
    rows, width = tokens_in.shape
    half_rows = rows // 2
    slab = query_weight.shape[0]
    query_columns = query_weight.shape[1]
    key_columns = key_weight.shape[1]
    hidden = gate_weight.shape[1] // nf
    half_hidden = hidden // 2
    local_groups = key_columns // HEAD_DIM
    group_size = HEADS // KV_HEADS
    group_width = group_size * HEAD_DIM
    score_scale = HEAD_DIM ** (-0.5)

    def my_half(array):
        return lax.dynamic_slice_in_dim(array, core * half_rows, half_rows, 0)

    def tp_order(mine, other):
        here = core == 0
        return jnp.where(here, mine, other), jnp.where(here, other, mine)

    def tp_sum(partial):
        return partial + swap_pair(partial, "tp")

    def plane_rows(array):
        mine = jnp.concatenate(plane.gather(my_half(array)), axis=0)
        return jnp.concatenate([mine, swap_pair(mine, "tp")], axis=0)

    def plane_columns(array):
        blocks = my_half(array).reshape(half_rows, far, 2, slab).transpose(1, 2, 0, 3)
        got = plane.all_to_all(blocks, high, low)
        ordered = jnp.stack(got)
        first = jnp.where(low == 0, ordered[:, 0], ordered[:, 1])
        second = jnp.where(low == 0, ordered[:, 1], ordered[:, 0])
        mine = jnp.stack([first, second], axis=1).reshape(nf, half_rows, slab)
        one, two = tp_order(mine, swap_pair(mine, "tp"))
        return jnp.stack([one, two], axis=1).reshape(nf * rows, slab)

    gain_rows = jnp.zeros((8, query_columns + 2 * key_columns), BF16)
    gain_rows = gain_rows.at[0, :slab].set(attn_gain).at[1, :slab].set(mlp_gain)
    qkv_shard = jnp.concatenate(
        [jnp.concatenate([query_weight, key_weight, value_weight], axis=1), gain_rows], axis=0
    )
    qkv_blocks = plane.gather(qkv_shard)
    qkv_full = place([b[:slab] for b in qkv_blocks], me, nf, 0)
    gains = place([b[slab : slab + 2, :slab] for b in qkv_blocks], me, nf, 1).astype(F32)
    gain_one, gain_two = gains[0:1], gains[1:2]
    output_full = place(plane.gather(output_weight), me, nf, 0)

    mlp_shard = jnp.stack([gate_weight.T, up_weight.T, down_weight.T])
    mlp_halves = mlp_shard.reshape(3, nf, 2, half_hidden, slab)
    mlp_sent = jnp.where(ctx == 0, mlp_halves[:, :, 0], mlp_halves[:, :, 1])
    mlp_sent = mlp_sent.reshape(3, far, 2, half_hidden, slab).transpose(1, 2, 0, 3, 4)
    mlp_got = plane.all_to_all(mlp_sent, high, low)
    mlp_mine = place(
        [b.transpose(1, 2, 0, 3).reshape(3, half_hidden, 2 * slab) for b in mlp_got],
        high,
        far,
        2,
    )
    mlp_all = jnp.concatenate([mlp_mine, swap_pair(mlp_mine, "ctx")], axis=1)
    gate_t, up_t, down_t = mlp_all[0], mlp_all[1], mlp_all[2]

    tokens = tokens_in.astype(F32)
    rms_one = lax.rsqrt(jnp.mean(tokens * tokens, axis=-1, keepdims=True) + EPSILON)
    scaled_one = tokens * rms_one
    normed_one = (scaled_one * gain_one).astype(BF16)
    qkv_lin = dot_nn(normed_one, qkv_full)
    query_lin = qkv_lin[:, :query_columns]
    key_lin = qkv_lin[:, query_columns : query_columns + key_columns]
    value_lin = qkv_lin[:, query_columns + key_columns :]
    cosine_table, sine_table = rotary_tables(doc_positions)
    queries = (
        apply_rotary(query_lin.reshape(rows, -1, HEAD_DIM), cosine_table, sine_table)
        .astype(BF16)
        .reshape(rows, query_columns)
    )
    keys_low = (
        apply_rotary(key_lin.reshape(rows, -1, HEAD_DIM), cosine_table, sine_table)
        .astype(BF16)
        .reshape(rows, key_columns)
    )
    values_low = value_lin.astype(BF16)
    kv_mine = jnp.concatenate([keys_low, values_low], axis=1)
    kv_all = jnp.concatenate([kv_mine, swap_pair(kv_mine, "ctx")], axis=0)
    key_all, value_all = kv_all[:, :key_columns], kv_all[:, key_columns:]
    places = jnp.arange(rows, dtype=jnp.int32)
    query_places = ctx * rows + places
    key_places = jnp.concatenate([ctx * rows + places, (1 - ctx) * rows + places])
    allowed = (key_places[None, :] <= query_places[:, None]) & (
        key_places[None, :] >= (query_places - doc_positions)[:, None]
    )

    def head_scores(query_group, key_head):
        raw_scores = (
            jnp.einsum("ngd,kd->gnk", query_group, key_head, preferred_element_type=F32)
            * score_scale
        )
        return jnp.where(allowed[None], raw_scores, NEG_FILL)

    attended_parts = []
    lse_parts = []
    for group_index in range(local_groups):
        query_group = queries[
            :, group_index * group_width : (group_index + 1) * group_width
        ].reshape(rows, group_size, HEAD_DIM)
        key_head = key_all[:, group_index * HEAD_DIM : (group_index + 1) * HEAD_DIM]
        value_head = value_all[:, group_index * HEAD_DIM : (group_index + 1) * HEAD_DIM]
        scores = head_scores(query_group, key_head)
        largest = jnp.max(scores, axis=-1, keepdims=True)
        exponent = jnp.exp(scores - largest)
        totals = jnp.sum(exponent, axis=-1, keepdims=True)
        probs_low = (exponent / totals).astype(BF16)
        attended_parts.append(
            jnp.einsum("gnk,kd->ngd", probs_low, value_head, preferred_element_type=F32).reshape(
                rows, group_width
            )
        )
        lse_parts.append(largest + jnp.log(totals))
    attended_low = jnp.concatenate(attended_parts, axis=1).astype(BF16)
    residual = tokens + tp_sum(dot_nt(attended_low, output_full))
    rms_two = lax.rsqrt(jnp.mean(residual * residual, axis=-1, keepdims=True) + EPSILON)
    scaled_two = residual * rms_two
    normed_two = (scaled_two * gain_two).astype(BF16)

    cot_all = plane_rows(cotangent)
    grad_act = dot_nt(cot_all, down_t)
    normed_all = plane_rows(normed_two)
    gate_lin = dot_nt(normed_all, gate_t)
    up_lin = dot_nt(normed_all, up_t)
    sigmoid = 1.0 / (1.0 + jnp.exp(-gate_lin))
    silu_value = gate_lin / (1.0 + jnp.exp(-gate_lin))
    act_low = (silu_value * up_lin).astype(BF16)
    grad_gate_lin = (grad_act * up_lin * sigmoid * (1.0 + gate_lin * (1.0 - sigmoid))).astype(BF16)
    grad_up_lin = (grad_act * silu_value).astype(BF16)

    def token_sum(partial, wire):
        here = partial[0] + swap_pair(partial[1].astype(wire), "tp").astype(F32)
        return plane.reduce([here[k] for k in range(nf)], wire)

    def both_halves(mine):
        one, two = tp_order(mine, swap_pair(mine, "tp"))
        return jnp.concatenate([one, two], axis=0)

    grad_normed_two = both_halves(
        token_sum(
            (dot_nn(grad_gate_lin, gate_t) + dot_nn(grad_up_lin, up_t)).reshape(
                2, nf, half_rows, width
            ),
            F32,
        )
    )
    mlp_branch = both_halves(
        token_sum(dot_nn(act_low, down_t).reshape(2, nf, half_rows, width), BF16)
    )
    block_out = (residual + mlp_branch).astype(BF16)

    grad_out = cotangent.astype(F32)
    scaled_grad_two = grad_normed_two * gain_two
    grad_residual = (
        grad_out
        + rms_two * scaled_grad_two
        - residual
        * (rms_two * rms_two * rms_two)
        * jnp.mean(scaled_grad_two * residual, axis=-1, keepdims=True)
    )
    grad_attn_low = grad_residual.astype(BF16)
    grad_attended = dot_nn(grad_attn_low, output_full).astype(BF16)
    query_grads = []
    key_grads = []
    value_grads = []
    for group_index in range(local_groups):
        query_group = queries[
            :, group_index * group_width : (group_index + 1) * group_width
        ].reshape(rows, group_size, HEAD_DIM)
        key_head = key_all[:, group_index * HEAD_DIM : (group_index + 1) * HEAD_DIM]
        value_head = value_all[:, group_index * HEAD_DIM : (group_index + 1) * HEAD_DIM]
        probabilities = jnp.exp(head_scores(query_group, key_head) - lse_parts[group_index])
        probs_low = probabilities.astype(BF16)
        grad_group = grad_attended[
            :, group_index * group_width : (group_index + 1) * group_width
        ].reshape(rows, group_size, HEAD_DIM)
        grad_probs = jnp.einsum("ngd,kd->gnk", grad_group, value_head, preferred_element_type=F32)
        row_dot = jnp.sum(probabilities * grad_probs, axis=-1, keepdims=True)
        grad_scores = (probabilities * (grad_probs - row_dot)).astype(BF16)
        query_grads.append(
            jnp.einsum("gnk,kd->ngd", grad_scores, key_head, preferred_element_type=F32)
            * score_scale
        )
        key_grads.append(
            jnp.einsum("gnk,ngd->kd", grad_scores, query_group, preferred_element_type=F32)
            * score_scale
        )
        value_grads.append(
            jnp.einsum("gnk,ngd->kd", probs_low, grad_group, preferred_element_type=F32)
        )
    kv_grads = jnp.concatenate(key_grads + value_grads, axis=1)
    kv_grad_local = kv_grads[:rows] + swap_pair(kv_grads[rows:], "ctx")
    key_grad_local, value_grad_local = kv_grad_local[:, :key_columns], kv_grad_local[:, key_columns:]
    grad_q_lin = (
        undo_rotary(jnp.concatenate(query_grads, axis=1), cosine_table, sine_table)
        .astype(BF16)
        .reshape(rows, query_columns)
    )
    grad_k_lin = (
        undo_rotary(key_grad_local.reshape(rows, -1, HEAD_DIM), cosine_table, sine_table)
        .astype(BF16)
        .reshape(rows, key_columns)
    )
    grad_qkv_lin = jnp.concatenate(
        [grad_q_lin, grad_k_lin, value_grad_local.astype(BF16)], axis=1
    )
    grad_normed_one = tp_sum(dot_nt(grad_qkv_lin, qkv_full))
    scaled_grad_one = grad_normed_one * gain_one
    grad_tokens = (
        grad_residual
        + rms_one * scaled_grad_one
        - tokens
        * (rms_one * rms_one * rms_one)
        * jnp.mean(scaled_grad_one * tokens, axis=-1, keepdims=True)
    )

    grad_qkv = dot_tn(
        plane_columns(normed_one), jnp.concatenate(plane.gather(grad_qkv_lin), axis=0)
    )
    grad_wo = dot_tn(
        plane_columns(grad_attn_low), jnp.concatenate(plane.gather(attended_low), axis=0)
    )
    proj = jnp.concatenate([grad_qkv, grad_wo], axis=1)
    proj = proj + swap_pair(proj, "ctx")
    query_grad = proj[:, :query_columns]
    key_grad = proj[:, query_columns : query_columns + key_columns]
    value_grad = proj[:, query_columns + key_columns : query_columns + 2 * key_columns]
    output_grad = proj[:, query_columns + 2 * key_columns :]

    grads_t = jnp.stack(
        [dot_tn(grad_gate_lin, normed_all), dot_tn(grad_up_lin, normed_all), dot_tn(act_low, cot_all)]
    ).reshape(3, 2, half_hidden, width)
    half_t = grads_t[:, 0] + swap_pair(grads_t[:, 1], "ctx")
    blocks_t = half_t.reshape(3 * half_hidden, far, 2, slab).transpose(1, 2, 0, 3)
    got_t = plane.all_to_all(blocks_t, high, low)
    mine_t = place(got_t, high, far, 0)
    other_t = swap_pair(mine_t, "ctx")
    here = ctx == 0
    whole_t = jnp.stack(
        [jnp.where(here, mine_t, other_t), jnp.where(here, other_t, mine_t)], axis=1
    ).reshape(nf, 2, 3, half_hidden, slab)
    mlp_grads = [whole_t[:, :, i].reshape(nf * hidden, slab).T for i in range(3)]

    gain_sums = lax.psum(
        jnp.stack(
            [
                jnp.sum(grad_normed_one * scaled_one, axis=0),
                jnp.sum(grad_normed_two * scaled_two, axis=0),
            ]
        ),
        ("fsdp", "ctx"),
    )
    gain_sums = lax.dynamic_slice_in_dim(gain_sums, me * slab, slab, 1)
    return (
        block_out,
        grad_tokens,
        gain_sums[0],
        query_grad,
        key_grad,
        value_grad,
        output_grad,
        gain_sums[1],
        mlp_grads[0],
        mlp_grads[1],
        mlp_grads[2],
    )


def contract_last(left_array, right_array):
    return lax.dot_general(
        left_array, right_array, (((1,), (1,)), ((), ())), preferred_element_type=F32
    )


def contract_first(left_array, right_array):
    return lax.dot_general(
        left_array, right_array, (((0,), (0,)), ((), ())), preferred_element_type=F32
    )


def normed_fold(scaled, pieces):
    gain_float = pieces[0].astype(F32)
    normed = (scaled * gain_float[None, :]).astype(BF16)
    sums = tuple(
        (jnp.dot(normed, matrix, preferred_element_type=F32) for matrix in pieces[1:])
    )
    return sums + (normed, gain_float)


def row_fold(left_array, shard_piece):
    return jnp.dot(left_array, shard_piece, preferred_element_type=F32)


def column_fold(gradients_in, pieces):
    part_sum = contract_last(gradients_in[0], pieces[0])
    for grad_piece, weight_piece in zip(gradients_in[1:], pieces[1:]):
        part_sum = part_sum + contract_last(grad_piece, weight_piece)
    return part_sum


def column_map(left_array, shard_piece):
    return contract_last(left_array, shard_piece)


def tensor_total(partial_sum):
    return lax.psum(partial_sum, "tp")


def rows_body(
    tokens_in,
    doc_positions,
    attn_gain,
    query_weight,
    key_weight,
    value_weight,
    output_weight,
    mlp_gain,
    gate_weight,
    up_weight,
    down_weight,
    cotangent,
):
    local_rows = tokens_in.shape[0]
    query_columns = query_weight.shape[1]
    key_columns = key_weight.shape[1]
    local_groups = key_columns // HEAD_DIM
    group_size = HEADS // KV_HEADS
    group_width = group_size * HEAD_DIM
    score_scale = HEAD_DIM ** (-0.5)
    tokens = tokens_in.astype(F32)
    rms_one = lax.rsqrt(jnp.mean(tokens * tokens, axis=-1, keepdims=True) + EPSILON)
    scaled_one = tokens * rms_one
    query_lin, key_lin, value_lin, normed_one, gain_one = normed_fold(
        scaled_one,
        (
            lax.all_gather(attn_gain, "fsdp", axis=0, tiled=True),
            lax.all_gather(query_weight, "fsdp", axis=0, tiled=True),
            lax.all_gather(key_weight, "fsdp", axis=0, tiled=True),
            lax.all_gather(value_weight, "fsdp", axis=0, tiled=True),
        ),
    )
    cosine_table, sine_table = rotary_tables(doc_positions)
    queries = (
        apply_rotary(query_lin.reshape(local_rows, -1, HEAD_DIM), cosine_table, sine_table)
        .astype(BF16)
        .reshape(local_rows, query_columns)
    )
    keys_low = (
        apply_rotary(key_lin.reshape(local_rows, -1, HEAD_DIM), cosine_table, sine_table)
        .astype(BF16)
        .reshape(local_rows, key_columns)
    )
    values_low = value_lin.astype(BF16)
    key_all, value_all = (
        lax.all_gather(keys_low, "ctx", axis=0, tiled=True),
        lax.all_gather(values_low, "ctx", axis=0, tiled=True),
    )
    key_count = key_all.shape[0]
    query_places = lax.axis_index("ctx") * local_rows + jnp.arange(local_rows, dtype=jnp.int32)
    key_places = jnp.arange(key_count, dtype=jnp.int32)
    allowed = (key_places[None, :] <= query_places[:, None]) & (
        key_places[None, :] >= (query_places - doc_positions)[:, None]
    )

    def head_scores(query_group, key_head):
        raw_scores = (
            jnp.einsum("ngd,kd->gnk", query_group, key_head, preferred_element_type=F32)
            * score_scale
        )
        return jnp.where(allowed[None], raw_scores, NEG_FILL)

    attended_parts = []
    lse_parts = []
    for group_index in range(local_groups):
        query_group = queries[
            :, group_index * group_width : (group_index + 1) * group_width
        ].reshape(local_rows, group_size, HEAD_DIM)
        key_head = key_all[:, group_index * HEAD_DIM : (group_index + 1) * HEAD_DIM]
        value_head = value_all[:, group_index * HEAD_DIM : (group_index + 1) * HEAD_DIM]
        scores = head_scores(query_group, key_head)
        largest = jnp.max(scores, axis=-1, keepdims=True)
        exponent = jnp.exp(scores - largest)
        totals = jnp.sum(exponent, axis=-1, keepdims=True)
        probs_low = (exponent / totals).astype(BF16)
        attended_parts.append(
            jnp.einsum(
                "gnk,kd->ngd", probs_low, value_head, preferred_element_type=F32
            ).reshape(local_rows, group_width)
        )
        lse_parts.append(largest + jnp.log(totals))
    attended_low = jnp.concatenate(attended_parts, axis=1).astype(BF16)
    attn_branch = tensor_total(
        column_map(attended_low, lax.all_gather(output_weight, "fsdp", axis=0, tiled=True))
    )
    residual = tokens + attn_branch
    rms_two = lax.rsqrt(jnp.mean(residual * residual, axis=-1, keepdims=True) + EPSILON)
    scaled_two = residual * rms_two
    gate_lin, up_lin, normed_two, gain_two = normed_fold(
        scaled_two,
        (
            lax.all_gather(mlp_gain, "fsdp", axis=0, tiled=True),
            lax.all_gather(gate_weight, "fsdp", axis=0, tiled=True),
            lax.all_gather(up_weight, "fsdp", axis=0, tiled=True),
        ),
    )
    silu_value = gate_lin / (1.0 + jnp.exp(-gate_lin))
    act_low = (silu_value * up_lin).astype(BF16)
    mlp_branch = tensor_total(
        column_map(act_low, lax.all_gather(down_weight, "fsdp", axis=0, tiled=True))
    )
    block_out = (residual + mlp_branch).astype(BF16)
    grad_out = cotangent.astype(F32)
    grad_act = row_fold(cotangent, lax.all_gather(down_weight, "fsdp", axis=0, tiled=True))
    sigmoid = 1.0 / (1.0 + jnp.exp(-gate_lin))
    grad_gate_lin = (grad_act * up_lin * sigmoid * (1.0 + gate_lin * (1.0 - sigmoid))).astype(
        BF16
    )
    grad_up_lin = (grad_act * silu_value).astype(BF16)
    grad_normed_two = tensor_total(
        column_fold(
            (grad_gate_lin, grad_up_lin),
            (
                lax.all_gather(gate_weight, "fsdp", axis=0, tiled=True),
                lax.all_gather(up_weight, "fsdp", axis=0, tiled=True),
            ),
        )
    )
    scaled_grad_two = grad_normed_two * gain_two[None, :]
    grad_residual = (
        grad_out
        + rms_two * scaled_grad_two
        - residual
        * (rms_two * rms_two * rms_two)
        * jnp.mean(scaled_grad_two * residual, axis=-1, keepdims=True)
    )
    grad_attn_low = grad_residual.astype(BF16)
    grad_attended = row_fold(
        grad_attn_low, lax.all_gather(output_weight, "fsdp", axis=0, tiled=True)
    ).astype(BF16)
    query_grads = []
    key_grads = []
    value_grads = []
    for group_index in range(local_groups):
        query_group = queries[
            :, group_index * group_width : (group_index + 1) * group_width
        ].reshape(local_rows, group_size, HEAD_DIM)
        key_head = key_all[:, group_index * HEAD_DIM : (group_index + 1) * HEAD_DIM]
        value_head = value_all[:, group_index * HEAD_DIM : (group_index + 1) * HEAD_DIM]
        probabilities = jnp.exp(head_scores(query_group, key_head) - lse_parts[group_index])
        probs_low = probabilities.astype(BF16)
        grad_group = grad_attended[
            :, group_index * group_width : (group_index + 1) * group_width
        ].reshape(local_rows, group_size, HEAD_DIM)
        grad_probs = jnp.einsum(
            "ngd,kd->gnk", grad_group, value_head, preferred_element_type=F32
        )
        row_dot = jnp.sum(probabilities * grad_probs, axis=-1, keepdims=True)
        grad_scores = (probabilities * (grad_probs - row_dot)).astype(BF16)
        query_grads.append(
            jnp.einsum("gnk,kd->ngd", grad_scores, key_head, preferred_element_type=F32)
            * score_scale
        )
        key_grads.append(
            jnp.einsum("gnk,ngd->kd", grad_scores, query_group, preferred_element_type=F32)
            * score_scale
        )
        value_grads.append(
            jnp.einsum("gnk,ngd->kd", probs_low, grad_group, preferred_element_type=F32)
        )
    key_grad_local, value_grad_local = (
        lax.psum_scatter(
            jnp.concatenate(key_grads, axis=1), "ctx", scatter_dimension=0, tiled=True
        ),
        lax.psum_scatter(
            jnp.concatenate(value_grads, axis=1), "ctx", scatter_dimension=0, tiled=True
        ),
    )
    grad_q_lin = (
        undo_rotary(jnp.concatenate(query_grads, axis=1), cosine_table, sine_table)
        .astype(BF16)
        .reshape(local_rows, query_columns)
    )
    grad_k_lin = (
        undo_rotary(key_grad_local.reshape(local_rows, -1, HEAD_DIM), cosine_table, sine_table)
        .astype(BF16)
        .reshape(local_rows, key_columns)
    )
    grad_v_lin = value_grad_local.astype(BF16)
    grad_normed_one = tensor_total(
        column_fold(
            (grad_q_lin, grad_k_lin, grad_v_lin),
            (
                lax.all_gather(query_weight, "fsdp", axis=0, tiled=True),
                lax.all_gather(key_weight, "fsdp", axis=0, tiled=True),
                lax.all_gather(value_weight, "fsdp", axis=0, tiled=True),
            ),
        )
    )
    scaled_grad_one = grad_normed_one * gain_one[None, :]
    grad_tokens = (
        grad_residual
        + rms_one * scaled_grad_one
        - tokens
        * (rms_one * rms_one * rms_one)
        * jnp.mean(scaled_grad_one * tokens, axis=-1, keepdims=True)
    )
    owned = lax.psum_scatter(
        (
            jnp.sum(grad_normed_one * scaled_one, axis=0),
            contract_first(normed_one, grad_q_lin),
            contract_first(normed_one, grad_k_lin),
            contract_first(normed_one, grad_v_lin),
            contract_first(grad_attn_low, attended_low),
            jnp.sum(grad_normed_two * scaled_two, axis=0),
            contract_first(normed_two, grad_gate_lin),
            contract_first(normed_two, grad_up_lin),
            contract_first(cotangent, act_low),
        ),
        "fsdp",
        scatter_dimension=0,
        tiled=True,
    )
    (
        gain_one_grad,
        query_grad,
        key_grad,
        value_grad,
        output_grad,
        gain_two_grad,
        gate_grad,
        up_grad,
        down_grad,
    ) = owned
    summed = lax.psum(
        (
            gain_one_grad,
            query_grad,
            key_grad,
            value_grad,
            output_grad,
            gain_two_grad,
            gate_grad,
            up_grad,
            down_grad,
        ),
        "ctx",
    )
    return (
        block_out,
        grad_tokens,
        summed[0],
        summed[1],
        summed[2],
        summed[3],
        summed[4],
        summed[5],
        summed[6],
        summed[7],
        summed[8],
    )


def choose_body(plane, *arrays):
    rows, width = arrays[0].shape
    if plane.size * rows <= width:
        return body(plane, *arrays)
    return rows_body(*arrays)


def solution(mesh):
    rows = P(("fsdp", "ctx"), None)
    weight = P("fsdp", "tp")
    gain = P("fsdp")
    return jax.shard_map(
        functools.partial(choose_body, Plane(mesh.shape["fsdp"])),
        mesh=mesh,
        in_specs=(
            rows,
            P(("fsdp", "ctx")),
            gain,
            weight,
            weight,
            weight,
            weight,
            gain,
            weight,
            weight,
            weight,
            rows,
        ),
        out_specs=(rows, rows, gain, weight, weight, weight, weight, gain, weight, weight, weight),
        check_vma=False,
    )
```

```python
import functools

import jax
import jax.numpy as jnp
from jax import lax
from jax.experimental import pallas as pl
from jax.experimental.pallas import tpu as pltpu
from jax.sharding import PartitionSpec as P


HEADS = 32
KV_HEADS = 4
HEAD_DIM = 64

EPSILON = 1e-05
NEG_FILL = -1e30


F32 = jnp.float32
BF16 = jnp.bfloat16


def rotary_tables(positions):
    half_dim = HEAD_DIM // 2
    inverse = 1.0 / 10000.0 ** (jnp.arange(half_dim, dtype=F32) * (2.0 / HEAD_DIM))
    angles = positions.astype(F32)[:, None] * inverse[None, :]
    cosine_table = jnp.concatenate([jnp.cos(angles), jnp.cos(angles)], axis=-1)[:, None, :]
    sine_table = jnp.concatenate([jnp.sin(angles), jnp.sin(angles)], axis=-1)[:, None, :]
    return (cosine_table, sine_table)


def apply_rotary(values, cosine_table, sine_table):
    half_dim = values.shape[-1] // 2
    turned = jnp.concatenate([-values[..., half_dim:], values[..., :half_dim]], axis=-1)
    return values * cosine_table + turned * sine_table


def undo_rotary(gradient, cosine_table, sine_table):
    half_dim = gradient.shape[-1] // 2
    sined = gradient * sine_table
    return gradient * cosine_table + jnp.concatenate(
        [sined[..., half_dim:], -sined[..., :half_dim]], axis=-1
    )


def dot_nt(left, right):
    return lax.dot_general(left, right, (((1,), (1,)), ((), ())), preferred_element_type=F32)


def dot_tn(left, right):
    return lax.dot_general(left, right, (((0,), (0,)), ((), ())), preferred_element_type=F32)


def dot_nn(left, right):
    return jnp.dot(left, right, preferred_element_type=F32)


class Plane:
    def __init__(self, size):
        self.size = size
        self.far = size // 2

    def send(self, array, axis, pairs):
        return lax.ppermute(array, axis, pairs)

    def swap(self, array, step):
        pairs = [(i, i ^ step) for i in range(self.size)]
        return self.send(array, "fsdp", pairs)

    def swap_ctx(self, array):
        return self.send(array, "ctx", [(0, 1), (1, 0)])

    def swap_tp(self, array):
        return self.send(array, "tp", [(0, 1), (1, 0)])

    def sum_all(self, array):
        array = sum((self.swap(array, 2 * k) for k in range(1, self.far)), array)
        array = array + self.swap(array, 1)
        return array + self.swap_ctx(array)

    def gather_far(self, shard):
        far = [self.swap(shard, 2 * k) for k in range(1, self.far)]
        return [shard] + far

    def gather_near(self, blocks):
        out = []
        for block in blocks:
            out += [block, self.swap(block, 1)]
        return out

    def gather(self, shard):
        return self.gather_near(self.gather_far(shard))

    def exchange_near(self, blocks, low):
        here = low == 0
        kept = jnp.stack([jnp.where(here, a, b) for a, b in zip(blocks[0::2], blocks[1::2])])
        sent = jnp.stack([jnp.where(here, b, a) for a, b in zip(blocks[0::2], blocks[1::2])])
        return kept, self.swap(sent, 1)

    def exchange_far(self, kept, got, high):
        out = []
        for k in range(self.far):
            block = jnp.stack(
                [lax.dynamic_index_in_dim(b, high ^ k, 0, keepdims=False) for b in (kept, got)]
            )
            out.append(self.swap(block, 2 * k) if k else block)
        return out

    def reduce_near(self, chunk, wire=F32):
        chunk = chunk.reshape(self.far, 2, *chunk.shape[1:])
        sent = chunk[:, 1].astype(wire)
        return chunk[:, 0].astype(F32), self.swap(sent, 1)

    def reduce_far(self, sums, wire=F32):
        got = [self.swap(sums[k].astype(wire), 2 * k) for k in range(1, self.far)]
        return sum((g.astype(F32) for g in got), sums[0])


class Fences:
    def __init__(self, seed):
        self.value = seed

    def cut(self, *before):
        value, *before = lax.optimization_barrier((self.value, *before))
        self.value = value + 1
        return before[0] if len(before) == 1 else before

    def after(self, array):
        array, self.value = lax.optimization_barrier((array, self.value))
        return array


def place(blocks, index, size, axis):
    shape = list(blocks[0].shape)
    width = shape[axis]
    shape[axis] = width * size
    out = jnp.zeros(shape, blocks[0].dtype)
    for k, block in enumerate(blocks):
        out = lax.dynamic_update_slice_in_dim(out, block, (index ^ k) * width, axis)
    return out


def owned_kernel(far, count, half_hidden, place_ref, *refs):
    got, other = refs[:far], refs[far : 2 * far]
    outs, rows = refs[2 * far : 2 * far + count], refs[-1]
    high, low, ctx = place_ref[0], place_ref[1], place_ref[2]
    for i in range(count):
        for k in range(far):
            for r in range(2):
                owner = (high ^ k) * 2 + (low ^ r)
                first = pl.multiple_of((owner * 2 + ctx) * half_hidden, 8)
                second = pl.multiple_of((owner * 2 + 1 - ctx) * half_hidden, 8)
                rows[pl.ds(first, half_hidden), :] = got[k][r, i]
                rows[pl.ds(second, half_hidden), :] = other[k][r, i]
        for j in range(rows.shape[0] // 128):
            outs[i][:, j * 128 : (j + 1) * 128] = rows[j * 128 : (j + 1) * 128, :].T


WHOLE = pl.BlockSpec(memory_space=pltpu.VMEM)
SCALARS = pl.BlockSpec(memory_space=pltpu.SMEM)


def local_kernel(kernel, outs, scratch, *arrays):
    moved = sum(x.size * x.dtype.itemsize for x in (*arrays, *outs))
    return pl.pallas_call(
        kernel,
        out_shape=outs,
        in_specs=[SCALARS] + [WHOLE] * (len(arrays) - 1),
        out_specs=[WHOLE] * len(outs),
        scratch_shapes=scratch,
        compiler_params=pltpu.CompilerParams(vmem_limit_bytes=40 * 2**20),
        cost_estimate=pl.CostEstimate(flops=0, bytes_accessed=moved, transcendentals=0),
    )(*arrays)


def slab_of(where_ref, k, slab):
    return pl.ds(pl.multiple_of((where_ref[0] ^ k) * slab, 128), slab)


def project_in_kernel(slab, where_ref, tokens_ref, *refs):
    blocks, (lin_ref, normed_ref, gains_ref) = refs[:-3], refs[-3:]
    for k, block in enumerate(blocks):
        pair = block[slab : slab + 8, :slab].astype(F32)
        gains_ref[:, slab_of(where_ref, k, slab)] = pair
    tokens = tokens_ref[...].astype(F32)
    rms = lax.rsqrt(jnp.mean(tokens * tokens, axis=-1, keepdims=True) + EPSILON)
    normed_ref[...] = (tokens * rms * gains_ref[0:1, :]).astype(BF16)
    total = None
    for k, block in enumerate(blocks):
        part = dot_nn(normed_ref[:, slab_of(where_ref, k, slab)], block[:slab, :])
        total = part if total is None else total + part
    lin_ref[...] = total


def project_out_kernel(slab, where_ref, left_ref, *refs):
    blocks, out_ref = refs[:-1], refs[-1]
    for k, block in enumerate(blocks):
        out_ref[:, slab_of(where_ref, k, slab)] = dot_nt(left_ref[...], block[:slab, :])


def project_back_kernel(slab, where_ref, left_ref, *refs):
    blocks, out_ref = refs[:-1], refs[-1]
    total = None
    for k, block in enumerate(blocks):
        part = dot_nn(left_ref[:, slab_of(where_ref, k, slab)], block[:slab, :])
        total = part if total is None else total + part
    out_ref[...] = total.astype(out_ref.dtype)


def outer_kernel(half, where_ref, mine_ref, other_ref, *refs):
    blocks, out_ref = refs[:-1], refs[-1]
    here = pl.ds(pl.multiple_of(where_ref[1] * half, 16), half)
    there = pl.ds(pl.multiple_of((1 - where_ref[1]) * half, 16), half)
    total = None
    for k, block in enumerate(blocks):
        part = dot_tn(mine_ref[k], block[here, :]) + dot_tn(other_ref[k], block[there, :])
        total = part if total is None else total + part
    out_ref[...] = total


def owned(got, other, where):
    far = len(got)
    _, count, half_hidden, slab = got[0].shape
    total = far * 4 * half_hidden
    return local_kernel(
        functools.partial(owned_kernel, far, count, half_hidden),
        [jax.ShapeDtypeStruct((slab, total), F32)] * count,
        [pltpu.VMEM((total, slab), F32)],
        where,
        *got,
        *other,
    )


def layer(
    plane,
    tokens_in,
    doc_positions,
    attn_gain,
    query_weight,
    key_weight,
    value_weight,
    output_weight,
    mlp_gain,
    gate_weight,
    up_weight,
    down_weight,
    cotangent,
):
    nf = plane.size
    me = lax.axis_index("fsdp")
    high, low = me // 2, me % 2
    ctx = lax.axis_index("ctx")
    core = lax.axis_index("tp")
    rows, width = tokens_in.shape
    half_rows = rows // 2
    slab = query_weight.shape[0]
    query_columns = query_weight.shape[1]
    key_columns = key_weight.shape[1]
    hidden = gate_weight.shape[1] // nf
    half_hidden = hidden // 2
    local_groups = key_columns // HEAD_DIM
    group_size = HEADS // KV_HEADS
    group_width = group_size * HEAD_DIM
    score_scale = HEAD_DIM ** (-0.5)

    def my_half(array):
        return lax.dynamic_slice_in_dim(array, core * half_rows, half_rows, 0)

    def tp_order(mine, other):
        here = core == 0
        return jnp.where(here, mine, other), jnp.where(here, other, mine)

    def tp_sum(partial):
        return partial + plane.swap_tp(partial)

    def plane_rows(array):
        mine = jnp.concatenate(plane.gather(my_half(array)), axis=0)
        return jnp.concatenate([mine, plane.swap_tp(mine)], axis=0)

    def columns_near(array):
        mine = my_half(array)
        blocks = [mine[:, i * slab : (i + 1) * slab] for i in range(nf)]
        return plane.exchange_near(blocks, low)

    fences = Fences(doc_positions[0])

    gain_rows = jnp.zeros((8, query_columns + 2 * key_columns), BF16)
    gain_rows = gain_rows.at[0, :slab].set(attn_gain).at[1, :slab].set(mlp_gain)
    qkv_shard = jnp.concatenate(
        [jnp.concatenate([query_weight, key_weight, value_weight], axis=1), gain_rows], axis=0
    )
    qkv_blocks = plane.gather(qkv_shard)
    output_blocks = plane.gather(output_weight)
    cot_all = plane_rows(cotangent)

    mlp_shard = jnp.stack([gate_weight.T, up_weight.T, down_weight.T])
    mlp_halves = mlp_shard.reshape(3, nf, 2, half_hidden, slab)
    mlp_sent = jnp.where(ctx == 0, mlp_halves[:, :, 0], mlp_halves[:, :, 1])
    mlp_kept, mlp_got = plane.exchange_near([mlp_sent[:, i] for i in range(nf)], low)
    mlp_blocks = plane.exchange_far(mlp_kept, mlp_got, high)

    fences.cut()
    fences.cut()
    fences.cut()
    fences.cut()
    tokens = tokens_in.astype(F32)
    rms_one = lax.rsqrt(jnp.mean(tokens * tokens, axis=-1, keepdims=True) + EPSILON)
    scaled_one = tokens * rms_one
    where = jnp.stack([me, core]).astype(jnp.int32)
    qkv_lin, normed_one, gains = local_kernel(
        functools.partial(project_in_kernel, slab),
        [
            jax.ShapeDtypeStruct((rows, query_columns + 2 * key_columns), F32),
            jax.ShapeDtypeStruct((rows, width), BF16),
            jax.ShapeDtypeStruct((8, width), F32),
        ],
        [],
        where,
        tokens_in,
        *qkv_blocks,
    )
    gain_one, gain_two = gains[0:1], gains[1:2]

    def project_out(left, blocks):
        return local_kernel(
            functools.partial(project_out_kernel, slab),
            [jax.ShapeDtypeStruct((rows, width), F32)],
            [],
            where,
            left,
            *blocks,
        )[0]

    def outer(got, blocks):
        mine = jnp.concatenate(got)
        return local_kernel(
            functools.partial(outer_kernel, half_rows),
            [jax.ShapeDtypeStruct((slab, blocks[0].shape[1]), F32)],
            [],
            where,
            mine,
            plane.swap_tp(mine),
            *blocks,
        )[0]

    query_lin = qkv_lin[:, :query_columns]
    key_lin = qkv_lin[:, query_columns : query_columns + key_columns]
    value_lin = qkv_lin[:, query_columns + key_columns :]
    cosine_table, sine_table = rotary_tables(doc_positions)
    queries = (
        apply_rotary(query_lin.reshape(rows, -1, HEAD_DIM), cosine_table, sine_table)
        .astype(BF16)
        .reshape(rows, query_columns)
    )
    keys_low = (
        apply_rotary(key_lin.reshape(rows, -1, HEAD_DIM), cosine_table, sine_table)
        .astype(BF16)
        .reshape(rows, key_columns)
    )
    values_low = value_lin.astype(BF16)
    kv_mine = jnp.concatenate([keys_low, values_low], axis=1)
    kv_mine, queries = fences.cut(kv_mine, queries)
    kv_all = jnp.concatenate([kv_mine, plane.swap_ctx(kv_mine)], axis=0)
    key_all, value_all = kv_all[:, :key_columns], kv_all[:, key_columns:]
    places = jnp.arange(rows, dtype=jnp.int32)
    query_places = ctx * rows + places
    key_places = jnp.concatenate([ctx * rows + places, (1 - ctx) * rows + places])
    allowed = (key_places[None, :] <= query_places[:, None]) & (
        key_places[None, :] >= (query_places - doc_positions)[:, None]
    )

    def head_scores(query_group, key_head):
        raw_scores = (
            jnp.einsum("ngd,kd->gnk", query_group, key_head, preferred_element_type=F32)
            * score_scale
        )
        return jnp.where(allowed[None], raw_scores, NEG_FILL)

    attended_parts = []
    lse_parts = []
    for group_index in range(local_groups):
        query_group = queries[
            :, group_index * group_width : (group_index + 1) * group_width
        ].reshape(rows, group_size, HEAD_DIM)
        key_head = key_all[:, group_index * HEAD_DIM : (group_index + 1) * HEAD_DIM]
        value_head = value_all[:, group_index * HEAD_DIM : (group_index + 1) * HEAD_DIM]
        scores = head_scores(query_group, key_head)
        largest = jnp.max(scores, axis=-1, keepdims=True)
        exponent = jnp.exp(scores - largest)
        totals = jnp.sum(exponent, axis=-1, keepdims=True)
        probs_low = (exponent / totals).astype(BF16)
        attended_parts.append(
            jnp.einsum("gnk,kd->ngd", probs_low, value_head, preferred_element_type=F32).reshape(
                rows, group_width
            )
        )
        lse_parts.append(largest + jnp.log(totals))
    attended_low = jnp.concatenate(attended_parts, axis=1).astype(BF16)
    attended_low = fences.cut(attended_low)
    residual = tokens + tp_sum(project_out(attended_low, output_blocks))
    rms_two = lax.rsqrt(jnp.mean(residual * residual, axis=-1, keepdims=True) + EPSILON)
    scaled_two = residual * rms_two
    normed_two = (scaled_two * gain_two).astype(BF16)

    normed_all = plane_rows(normed_two)
    fences.cut()
    fences.cut()
    fences.cut()
    fences.cut()
    mlp_mine = place([b[r] for b in mlp_blocks for r in range(2)], me, nf, 2)
    mlp_all = jnp.concatenate([mlp_mine, plane.swap_ctx(mlp_mine)], axis=1)
    gate_t, up_t, down_t = mlp_all[0], mlp_all[1], mlp_all[2]
    attended_far = plane.gather_far(attended_low)
    normed_near = columns_near(normed_one)
    normed_got = plane.exchange_far(*normed_near, high)
    gate_lin = dot_nt(normed_all, gate_t)
    up_lin = dot_nt(normed_all, up_t)
    grad_act = dot_nt(cot_all, down_t)
    sigmoid = 1.0 / (1.0 + jnp.exp(-gate_lin))
    silu_value = gate_lin / (1.0 + jnp.exp(-gate_lin))
    act_low = (silu_value * up_lin).astype(BF16)
    grad_gate_lin = (grad_act * up_lin * sigmoid * (1.0 + gate_lin * (1.0 - sigmoid))).astype(BF16)
    grad_up_lin = (grad_act * silu_value).astype(BF16)

    def ctx_half(left, right):
        whole = dot_tn(left, right)
        return whole[:half_hidden], plane.swap_ctx(whole[half_hidden:])

    def owners_near(halves):
        blocks = [
            jnp.stack([h[:, i * slab : (i + 1) * slab] for h in halves]) for i in range(nf)
        ]
        return plane.exchange_near(blocks, low)

    def from_owners(got):
        other = [plane.swap_ctx(g) for g in got]
        where = jnp.stack([high, low, ctx]).astype(jnp.int32)
        return owned(got, other, where)

    def tp_part(terms, wire, columns):
        half = nf * half_rows
        mine, other = [
            sum(dot_nn(left[h * half : (h + 1) * half], right[:, columns]) for left, right in terms)
            for h in range(2)
        ]
        other = plane.swap_tp(other.astype(wire)).astype(F32)
        return plane.reduce_near((mine + other).reshape(nf, half_rows, -1), wire)

    def whole_rows(mine):
        one, two = tp_order(mine, plane.swap_tp(mine))
        return jnp.concatenate([one, two], axis=0)

    pieces = 4
    step = width // pieces
    near = []
    reduced = []

    def piece(i):
        near.append(
            tp_part(
                ((fences.after(grad_gate_lin), gate_t), (fences.after(grad_up_lin), up_t)),
                F32,
                slice(i * step, (i + 1) * step),
            )
        )

    def piece_far(i):
        reduced.append(plane.reduce_far(near[i][0] + near[i][1]))

    grad_gate_lin, grad_up_lin, act_low = fences.cut(grad_gate_lin, grad_up_lin, act_low)
    piece(0)
    piece(1)
    half_down = sum(ctx_half(fences.after(act_low), cot_all))
    fences.cut()
    piece_far(0)
    piece(2)
    half_gate = sum(ctx_half(fences.after(grad_gate_lin), normed_all))
    fences.cut()
    piece_far(1)
    piece(3)
    half_up = sum(ctx_half(fences.after(grad_up_lin), normed_all))
    fences.cut()
    piece_far(2)
    mlp_kept, mlp_odd = tp_part(((fences.after(act_low), down_t),), BF16, slice(None))
    down_near = owners_near([half_down])
    fences.cut()
    piece_far(3)
    gate_up_near = owners_near([half_gate, half_up])
    fences.cut()
    down_got = plane.exchange_far(*down_near, high)
    fences.cut()
    grad_normed_two = whole_rows(jnp.concatenate(reduced, axis=-1))
    fences.cut()
    grad_out = cotangent.astype(F32)
    scaled_grad_two = grad_normed_two * gain_two
    grad_residual = (
        grad_out
        + rms_two * scaled_grad_two
        - residual
        * (rms_two * rms_two * rms_two)
        * jnp.mean(scaled_grad_two * residual, axis=-1, keepdims=True)
    )
    grad_attn_low = grad_residual.astype(BF16)
    grad_attended = local_kernel(
        functools.partial(project_back_kernel, slab),
        [jax.ShapeDtypeStruct((rows, query_columns), BF16)],
        [],
        where,
        grad_attn_low,
        *output_blocks,
    )[0]
    grad_attn_near = columns_near(grad_attn_low)
    grad_attended = fences.cut(grad_attended)
    query_grads = []
    key_grads = []
    value_grads = []
    for group_index in range(local_groups):
        query_group = queries[
            :, group_index * group_width : (group_index + 1) * group_width
        ].reshape(rows, group_size, HEAD_DIM)
        key_head = key_all[:, group_index * HEAD_DIM : (group_index + 1) * HEAD_DIM]
        value_head = value_all[:, group_index * HEAD_DIM : (group_index + 1) * HEAD_DIM]
        probabilities = jnp.exp(head_scores(query_group, key_head) - lse_parts[group_index])
        probs_low = probabilities.astype(BF16)
        grad_group = grad_attended[
            :, group_index * group_width : (group_index + 1) * group_width
        ].reshape(rows, group_size, HEAD_DIM)
        grad_probs = jnp.einsum("ngd,kd->gnk", grad_group, value_head, preferred_element_type=F32)
        row_dot = jnp.sum(probabilities * grad_probs, axis=-1, keepdims=True)
        grad_scores = (probabilities * (grad_probs - row_dot)).astype(BF16)
        query_grads.append(
            jnp.einsum("gnk,kd->ngd", grad_scores, key_head, preferred_element_type=F32)
            * score_scale
        )
        key_grads.append(
            jnp.einsum("gnk,ngd->kd", grad_scores, query_group, preferred_element_type=F32)
            * score_scale
        )
        value_grads.append(
            jnp.einsum("gnk,ngd->kd", probs_low, grad_group, preferred_element_type=F32)
        )
    kv_grads = jnp.concatenate(key_grads + value_grads, axis=1)
    kv_grads, *query_grads = fences.cut(kv_grads, *query_grads)
    mlp_mine = plane.reduce_far(mlp_kept + mlp_odd.astype(F32), BF16)
    grad_attn_got = plane.exchange_far(*grad_attn_near, high)
    kv_grad_local = kv_grads[:rows] + plane.swap_ctx(kv_grads[rows:])
    key_grad_local, value_grad_local = kv_grad_local[:, :key_columns], kv_grad_local[:, key_columns:]
    grad_q_lin = (
        undo_rotary(jnp.concatenate(query_grads, axis=1), cosine_table, sine_table)
        .astype(BF16)
        .reshape(rows, query_columns)
    )
    grad_k_lin = (
        undo_rotary(key_grad_local.reshape(rows, -1, HEAD_DIM), cosine_table, sine_table)
        .astype(BF16)
        .reshape(rows, key_columns)
    )
    grad_qkv_lin = jnp.concatenate(
        [grad_q_lin, grad_k_lin, value_grad_local.astype(BF16)], axis=1
    )
    grad_qkv_all = plane.gather(grad_qkv_lin)
    fences.cut()
    gate_up_got = plane.exchange_far(*gate_up_near, high)
    attended_all = plane.gather_near(attended_far)
    grad_normed_one = tp_sum(project_out(fences.after(grad_qkv_lin), qkv_blocks))
    fences.cut()
    gain_sums = plane.sum_all(
        jnp.stack(
            [
                jnp.sum(grad_normed_one * scaled_one, axis=0),
                jnp.sum(grad_normed_two * scaled_two, axis=0),
            ]
        ),
    )
    fences.cut()
    grad_wo = outer(grad_attn_got, [fences.after(b) for b in attended_all])
    fences.cut()
    grad_qkv = outer(normed_got, [fences.after(b) for b in grad_qkv_all])
    fences.cut()
    fences.cut()
    fences.cut()
    scaled_grad_one = grad_normed_one * gain_one
    grad_tokens = (
        grad_residual
        + rms_one * scaled_grad_one
        - tokens
        * (rms_one * rms_one * rms_one)
        * jnp.mean(scaled_grad_one * tokens, axis=-1, keepdims=True)
    )

    output_grad = grad_wo + plane.swap_ctx(grad_wo)
    block_out = (fences.after(residual) + whole_rows(mlp_mine)).astype(BF16)
    grad_qkv = grad_qkv + plane.swap_ctx(grad_qkv)
    query_grad = grad_qkv[:, :query_columns]
    key_grad = grad_qkv[:, query_columns : query_columns + key_columns]
    value_grad = grad_qkv[:, query_columns + key_columns :]
    (down_grad,) = from_owners(down_got)
    gate_grad, up_grad = from_owners(gate_up_got)

    gain_sums = lax.dynamic_slice_in_dim(gain_sums, me * slab, slab, 1)
    gain_sums = jnp.where(fences.value > 0, gain_sums, 0.0)
    return (
        block_out,
        grad_tokens,
        gain_sums[0],
        query_grad,
        key_grad,
        value_grad,
        output_grad,
        gain_sums[1],
        gate_grad,
        up_grad,
        down_grad,
    )


def contract_last(left_array, right_array):
    return lax.dot_general(
        left_array, right_array, (((1,), (1,)), ((), ())), preferred_element_type=F32
    )


def contract_first(left_array, right_array):
    return lax.dot_general(
        left_array, right_array, (((0,), (0,)), ((), ())), preferred_element_type=F32
    )


def normed_fold(scaled, pieces):
    gain_float = pieces[0].astype(F32)
    normed = (scaled * gain_float[None, :]).astype(BF16)
    sums = tuple(
        (jnp.dot(normed, matrix, preferred_element_type=F32) for matrix in pieces[1:])
    )
    return sums + (normed, gain_float)


def row_fold(left_array, shard_piece):
    return jnp.dot(left_array, shard_piece, preferred_element_type=F32)


def column_fold(gradients_in, pieces):
    part_sum = contract_last(gradients_in[0], pieces[0])
    for grad_piece, weight_piece in zip(gradients_in[1:], pieces[1:]):
        part_sum = part_sum + contract_last(grad_piece, weight_piece)
    return part_sum


def column_map(left_array, shard_piece):
    return contract_last(left_array, shard_piece)


def tensor_total(partial_sum):
    return lax.psum(partial_sum, "tp")


def rows_body(
    tokens_in,
    doc_positions,
    attn_gain,
    query_weight,
    key_weight,
    value_weight,
    output_weight,
    mlp_gain,
    gate_weight,
    up_weight,
    down_weight,
    cotangent,
):
    local_rows = tokens_in.shape[0]
    query_columns = query_weight.shape[1]
    key_columns = key_weight.shape[1]
    local_groups = key_columns // HEAD_DIM
    group_size = HEADS // KV_HEADS
    group_width = group_size * HEAD_DIM
    score_scale = HEAD_DIM ** (-0.5)
    tokens = tokens_in.astype(F32)
    rms_one = lax.rsqrt(jnp.mean(tokens * tokens, axis=-1, keepdims=True) + EPSILON)
    scaled_one = tokens * rms_one
    query_lin, key_lin, value_lin, normed_one, gain_one = normed_fold(
        scaled_one,
        (
            lax.all_gather(attn_gain, "fsdp", axis=0, tiled=True),
            lax.all_gather(query_weight, "fsdp", axis=0, tiled=True),
            lax.all_gather(key_weight, "fsdp", axis=0, tiled=True),
            lax.all_gather(value_weight, "fsdp", axis=0, tiled=True),
        ),
    )
    cosine_table, sine_table = rotary_tables(doc_positions)
    queries = (
        apply_rotary(query_lin.reshape(local_rows, -1, HEAD_DIM), cosine_table, sine_table)
        .astype(BF16)
        .reshape(local_rows, query_columns)
    )
    keys_low = (
        apply_rotary(key_lin.reshape(local_rows, -1, HEAD_DIM), cosine_table, sine_table)
        .astype(BF16)
        .reshape(local_rows, key_columns)
    )
    values_low = value_lin.astype(BF16)
    key_all, value_all = (
        lax.all_gather(keys_low, "ctx", axis=0, tiled=True),
        lax.all_gather(values_low, "ctx", axis=0, tiled=True),
    )
    key_count = key_all.shape[0]
    query_places = lax.axis_index("ctx") * local_rows + jnp.arange(local_rows, dtype=jnp.int32)
    key_places = jnp.arange(key_count, dtype=jnp.int32)
    allowed = (key_places[None, :] <= query_places[:, None]) & (
        key_places[None, :] >= (query_places - doc_positions)[:, None]
    )

    def head_scores(query_group, key_head):
        raw_scores = (
            jnp.einsum("ngd,kd->gnk", query_group, key_head, preferred_element_type=F32)
            * score_scale
        )
        return jnp.where(allowed[None], raw_scores, NEG_FILL)

    attended_parts = []
    lse_parts = []
    for group_index in range(local_groups):
        query_group = queries[
            :, group_index * group_width : (group_index + 1) * group_width
        ].reshape(local_rows, group_size, HEAD_DIM)
        key_head = key_all[:, group_index * HEAD_DIM : (group_index + 1) * HEAD_DIM]
        value_head = value_all[:, group_index * HEAD_DIM : (group_index + 1) * HEAD_DIM]
        scores = head_scores(query_group, key_head)
        largest = jnp.max(scores, axis=-1, keepdims=True)
        exponent = jnp.exp(scores - largest)
        totals = jnp.sum(exponent, axis=-1, keepdims=True)
        probs_low = (exponent / totals).astype(BF16)
        attended_parts.append(
            jnp.einsum(
                "gnk,kd->ngd", probs_low, value_head, preferred_element_type=F32
            ).reshape(local_rows, group_width)
        )
        lse_parts.append(largest + jnp.log(totals))
    attended_low = jnp.concatenate(attended_parts, axis=1).astype(BF16)
    attn_branch = tensor_total(
        column_map(attended_low, lax.all_gather(output_weight, "fsdp", axis=0, tiled=True))
    )
    residual = tokens + attn_branch
    rms_two = lax.rsqrt(jnp.mean(residual * residual, axis=-1, keepdims=True) + EPSILON)
    scaled_two = residual * rms_two
    gate_lin, up_lin, normed_two, gain_two = normed_fold(
        scaled_two,
        (
            lax.all_gather(mlp_gain, "fsdp", axis=0, tiled=True),
            lax.all_gather(gate_weight, "fsdp", axis=0, tiled=True),
            lax.all_gather(up_weight, "fsdp", axis=0, tiled=True),
        ),
    )
    silu_value = gate_lin / (1.0 + jnp.exp(-gate_lin))
    act_low = (silu_value * up_lin).astype(BF16)
    mlp_branch = tensor_total(
        column_map(act_low, lax.all_gather(down_weight, "fsdp", axis=0, tiled=True))
    )
    block_out = (residual + mlp_branch).astype(BF16)
    grad_out = cotangent.astype(F32)
    grad_act = row_fold(cotangent, lax.all_gather(down_weight, "fsdp", axis=0, tiled=True))
    sigmoid = 1.0 / (1.0 + jnp.exp(-gate_lin))
    grad_gate_lin = (grad_act * up_lin * sigmoid * (1.0 + gate_lin * (1.0 - sigmoid))).astype(
        BF16
    )
    grad_up_lin = (grad_act * silu_value).astype(BF16)
    grad_normed_two = tensor_total(
        column_fold(
            (grad_gate_lin, grad_up_lin),
            (
                lax.all_gather(gate_weight, "fsdp", axis=0, tiled=True),
                lax.all_gather(up_weight, "fsdp", axis=0, tiled=True),
            ),
        )
    )
    scaled_grad_two = grad_normed_two * gain_two[None, :]
    grad_residual = (
        grad_out
        + rms_two * scaled_grad_two
        - residual
        * (rms_two * rms_two * rms_two)
        * jnp.mean(scaled_grad_two * residual, axis=-1, keepdims=True)
    )
    grad_attn_low = grad_residual.astype(BF16)
    grad_attended = row_fold(
        grad_attn_low, lax.all_gather(output_weight, "fsdp", axis=0, tiled=True)
    ).astype(BF16)
    query_grads = []
    key_grads = []
    value_grads = []
    for group_index in range(local_groups):
        query_group = queries[
            :, group_index * group_width : (group_index + 1) * group_width
        ].reshape(local_rows, group_size, HEAD_DIM)
        key_head = key_all[:, group_index * HEAD_DIM : (group_index + 1) * HEAD_DIM]
        value_head = value_all[:, group_index * HEAD_DIM : (group_index + 1) * HEAD_DIM]
        probabilities = jnp.exp(head_scores(query_group, key_head) - lse_parts[group_index])
        probs_low = probabilities.astype(BF16)
        grad_group = grad_attended[
            :, group_index * group_width : (group_index + 1) * group_width
        ].reshape(local_rows, group_size, HEAD_DIM)
        grad_probs = jnp.einsum(
            "ngd,kd->gnk", grad_group, value_head, preferred_element_type=F32
        )
        row_dot = jnp.sum(probabilities * grad_probs, axis=-1, keepdims=True)
        grad_scores = (probabilities * (grad_probs - row_dot)).astype(BF16)
        query_grads.append(
            jnp.einsum("gnk,kd->ngd", grad_scores, key_head, preferred_element_type=F32)
            * score_scale
        )
        key_grads.append(
            jnp.einsum("gnk,ngd->kd", grad_scores, query_group, preferred_element_type=F32)
            * score_scale
        )
        value_grads.append(
            jnp.einsum("gnk,ngd->kd", probs_low, grad_group, preferred_element_type=F32)
        )
    key_grad_local, value_grad_local = (
        lax.psum_scatter(
            jnp.concatenate(key_grads, axis=1), "ctx", scatter_dimension=0, tiled=True
        ),
        lax.psum_scatter(
            jnp.concatenate(value_grads, axis=1), "ctx", scatter_dimension=0, tiled=True
        ),
    )
    grad_q_lin = (
        undo_rotary(jnp.concatenate(query_grads, axis=1), cosine_table, sine_table)
        .astype(BF16)
        .reshape(local_rows, query_columns)
    )
    grad_k_lin = (
        undo_rotary(key_grad_local.reshape(local_rows, -1, HEAD_DIM), cosine_table, sine_table)
        .astype(BF16)
        .reshape(local_rows, key_columns)
    )
    grad_v_lin = value_grad_local.astype(BF16)
    grad_normed_one = tensor_total(
        column_fold(
            (grad_q_lin, grad_k_lin, grad_v_lin),
            (
                lax.all_gather(query_weight, "fsdp", axis=0, tiled=True),
                lax.all_gather(key_weight, "fsdp", axis=0, tiled=True),
                lax.all_gather(value_weight, "fsdp", axis=0, tiled=True),
            ),
        )
    )
    scaled_grad_one = grad_normed_one * gain_one[None, :]
    grad_tokens = (
        grad_residual
        + rms_one * scaled_grad_one
        - tokens
        * (rms_one * rms_one * rms_one)
        * jnp.mean(scaled_grad_one * tokens, axis=-1, keepdims=True)
    )
    owned = lax.psum_scatter(
        (
            jnp.sum(grad_normed_one * scaled_one, axis=0),
            contract_first(normed_one, grad_q_lin),
            contract_first(normed_one, grad_k_lin),
            contract_first(normed_one, grad_v_lin),
            contract_first(grad_attn_low, attended_low),
            jnp.sum(grad_normed_two * scaled_two, axis=0),
            contract_first(normed_two, grad_gate_lin),
            contract_first(normed_two, grad_up_lin),
            contract_first(cotangent, act_low),
        ),
        "fsdp",
        scatter_dimension=0,
        tiled=True,
    )
    (
        gain_one_grad,
        query_grad,
        key_grad,
        value_grad,
        output_grad,
        gain_two_grad,
        gate_grad,
        up_grad,
        down_grad,
    ) = owned
    summed = lax.psum(
        (
            gain_one_grad,
            query_grad,
            key_grad,
            value_grad,
            output_grad,
            gain_two_grad,
            gate_grad,
            up_grad,
            down_grad,
        ),
        "ctx",
    )
    return (
        block_out,
        grad_tokens,
        summed[0],
        summed[1],
        summed[2],
        summed[3],
        summed[4],
        summed[5],
        summed[6],
        summed[7],
        summed[8],
    )


def choose_body(size, *arrays):
    rows, width = arrays[0].shape
    if size * rows <= width:
        return layer(Plane(size), *arrays)
    return rows_body(*arrays)


def solution(mesh):
    rows = P(("fsdp", "ctx"), None)
    weight = P("fsdp", "tp")
    gain = P("fsdp")
    return jax.shard_map(
        functools.partial(choose_body, mesh.shape["fsdp"]),
        mesh=mesh,
        in_specs=(
            rows,
            P(("fsdp", "ctx")),
            gain,
            weight,
            weight,
            weight,
            weight,
            gain,
            weight,
            weight,
            weight,
            rows,
        ),
        out_specs=(rows, rows, gain, weight, weight, weight, weight, gain, weight, weight, weight),
        check_vma=False,
    )
```

```python
import functools

import jax
import jax.numpy as jnp
from jax import lax
from jax.experimental import pallas as pl
from jax.experimental.pallas import tpu as pltpu
from jax.sharding import PartitionSpec as P


HEADS = 32
KV_HEADS = 4
HEAD_DIM = 64

EPSILON = 1e-05
NEG_FILL = -1e30


F32 = jnp.float32
BF16 = jnp.bfloat16


def pair_tables(positions):
    half_dim = HEAD_DIM // 2
    inverse = 1.0 / 10000.0 ** (jnp.arange(half_dim, dtype=F32) * (2.0 / HEAD_DIM))
    angles = positions.astype(F32)[:, None] * inverse[None, :]
    return jnp.tile(jnp.cos(angles), (1, 4)), jnp.tile(jnp.sin(angles), (1, 4))


def first_half(shape):
    return lax.broadcasted_iota(jnp.int32, shape, 1) % HEAD_DIM < HEAD_DIM // 2


def rope_pair(values, cosine, sine):
    span, half_dim = values.shape[1], HEAD_DIM // 2
    ahead, behind = pltpu.roll(values, span - half_dim, 1), pltpu.roll(values, half_dim, 1)
    return values * cosine + jnp.where(first_half(values.shape), -ahead, behind) * sine


def unrope_pair(gradient, cosine, sine):
    span, half_dim = gradient.shape[1], HEAD_DIM // 2
    sined = gradient * sine
    ahead, behind = pltpu.roll(sined, span - half_dim, 1), pltpu.roll(sined, half_dim, 1)
    return gradient * cosine + jnp.where(first_half(sined.shape), ahead, -behind)


def dot_nt(left, right):
    return lax.dot_general(left, right, (((1,), (1,)), ((), ())), preferred_element_type=F32)


def dot_tn(left, right):
    return lax.dot_general(left, right, (((0,), (0,)), ((), ())), preferred_element_type=F32)


def dot_nn(left, right):
    return jnp.dot(left, right, preferred_element_type=F32)


class Plane:
    def __init__(self, size):
        self.size = size
        self.far = size // 2

    def send(self, array, axis, pairs):
        return lax.ppermute(array, axis, pairs)

    def swap(self, array, step):
        pairs = [(i, i ^ step) for i in range(self.size)]
        return self.send(array, "fsdp", pairs)

    def swap_ctx(self, array):
        return self.send(array, "ctx", [(0, 1), (1, 0)])

    def swap_tp(self, array):
        return self.send(array, "tp", [(0, 1), (1, 0)])

    def sum_all(self, array):
        array = array + self.swap(array, 1)
        array = array + self.swap_ctx(array)
        return sum((self.swap(array, 2 * k) for k in range(1, self.far)), array)

    def gather_far(self, shard):
        far = [self.swap(shard, 2 * k) for k in range(1, self.far)]
        return [shard] + far

    def gather_near(self, blocks):
        out = []
        for block in blocks:
            out += [block, self.swap(block, 1)]
        return out

    def gather(self, shard):
        return self.gather_near(self.gather_far(shard))

    def gather_shared(self, shard, ctx, rows):
        first = shard.shape[0] - 2 * rows
        mine = jnp.where(ctx == 0, shard[first : first + rows], shard[first + rows :])
        blocks = self.gather(jnp.concatenate([shard[:first], mine]))
        groups = [(1, 2), (3, 4, 6), (5, 7)] if self.size == 8 else [range(1, self.size)]
        others = [None] * self.size
        for g, members in enumerate(groups):
            sent = jnp.stack([blocks[k][first:] for k in members])
            got = self.swap_ctx(sent)
            for j, k in enumerate(members):
                others[k] = (g, j)
            groups[g] = got
        return shard, blocks[1:], groups, others[1:]

    def exchange_near(self, blocks, low):
        here = low == 0
        kept = jnp.stack([jnp.where(here, a, b) for a, b in zip(blocks[0::2], blocks[1::2])])
        sent = jnp.stack([jnp.where(here, b, a) for a, b in zip(blocks[0::2], blocks[1::2])])
        return kept, self.swap(sent, 1)

    def exchange_far(self, kept, got, high):
        kept, high = lax.optimization_barrier((kept, high))
        out = []
        for k in range(self.far):
            block = jnp.stack(
                [lax.dynamic_index_in_dim(b, high ^ k, 0, keepdims=False) for b in (kept, got)]
            )
            out.append(self.swap(block, 2 * k) if k else block)
        return out

    def reduce_near(self, chunk, wire=F32):
        chunk = chunk.reshape(self.far, 2, *chunk.shape[1:])
        sent = chunk[:, 1].astype(wire)
        return chunk[:, 0].astype(F32), self.swap(sent, 1)

    def reduce_far(self, sums, wire=F32):
        got = [self.swap(sums[k].astype(wire), 2 * k) for k in range(1, self.far)]
        return sum((g.astype(F32) for g in got), sums[0])


class Fences:
    def __init__(self, seed):
        self.value = seed

    def cut(self, *before):
        value, *before = lax.optimization_barrier((self.value, *before))
        self.value = value + 1
        return before[0] if len(before) == 1 else before

    def after(self, array):
        array, self.value = lax.optimization_barrier((array, self.value))
        return array


def owned_kernel(far, count, half_hidden, place_ref, *refs):
    got, other = refs[:far], refs[far : 2 * far]
    outs, rows = refs[2 * far : 2 * far + count], refs[-1]
    high, low, ctx = place_ref[0], place_ref[1], place_ref[2]
    for i in range(count):
        for k in range(far):
            for r in range(2):
                owner = (high ^ k) * 2 + (low ^ r)
                first = pl.multiple_of((owner * 2 + ctx) * half_hidden, 8)
                second = pl.multiple_of((owner * 2 + 1 - ctx) * half_hidden, 8)
                rows[pl.ds(first, half_hidden), :] = got[k][r, i]
                rows[pl.ds(second, half_hidden), :] = other[k][r, i]
        for j in range(rows.shape[0] // 128):
            outs[i][:, j * 128 : (j + 1) * 128] = rows[j * 128 : (j + 1) * 128, :].T


WHOLE = pl.BlockSpec(memory_space=pltpu.VMEM)
SCALARS = pl.BlockSpec(memory_space=pltpu.SMEM)


def local_kernel(kernel, outs, scratch, *arrays):
    moved = sum(x.size * x.dtype.itemsize for x in (*arrays, *outs))
    return pl.pallas_call(
        kernel,
        out_shape=outs,
        in_specs=[SCALARS] + [WHOLE] * (len(arrays) - 1),
        out_specs=[WHOLE] * len(outs),
        scratch_shapes=scratch,
        compiler_params=pltpu.CompilerParams(vmem_limit_bytes=40 * 2**20),
        cost_estimate=pl.CostEstimate(flops=0, bytes_accessed=moved, transcendentals=0),
    )(*arrays)


def slab_of(where_ref, k, slab):
    return pl.ds(pl.multiple_of((where_ref[0] ^ k) * slab, 128), slab)


def assemble(where_ref, whole_ref, own, blocks, groups, others):
    rows = groups[0].shape[1]
    total = own.shape[0]
    first = total - 2 * rows
    here = pl.ds(pl.multiple_of(first + where_ref[2] * rows, 16), rows)
    there = pl.ds(pl.multiple_of(first + (1 - where_ref[2]) * rows, 16), rows)
    whole_ref[0] = own[...]
    for k, (block, (g, j)) in enumerate(zip(blocks, others)):
        whole_ref[k + 1, :first, :] = block[:first, :]
        whole_ref[k + 1, here, :] = block[first:, :]
        whole_ref[k + 1, there, :] = groups[g][j]


def split_refs(refs, others, outs):
    count = len(others)
    inputs = refs[: len(refs) - outs]
    return inputs[0], inputs[1 : 1 + count], inputs[1 + count :], refs[len(refs) - outs :]


def project_in_kernel(slab, others, where_ref, tokens_ref, cosine_ref, sine_ref, *refs):
    own, blocks, groups, outs = split_refs(refs, others, 5)
    query_ref, kv_ref, normed_ref, gains_ref, whole_ref = outs
    assemble(where_ref, whole_ref, own, blocks, groups, others)
    count = len(others) + 1
    for k in range(count):
        gains_ref[:, slab_of(where_ref, k, slab)] = whole_ref[k, slab:, :slab].astype(F32)
    tokens = tokens_ref[...].astype(F32)
    rms = lax.rsqrt(jnp.mean(tokens * tokens, axis=-1, keepdims=True) + EPSILON)
    normed_ref[...] = (tokens * rms * gains_ref[0:1, :]).astype(BF16)
    total = None
    for k in range(count):
        part = dot_nn(normed_ref[:, slab_of(where_ref, k, slab)], whole_ref[k, :slab, :])
        total = part if total is None else total + part
    cosine, sine = cosine_ref[...], sine_ref[...]
    queries, keys = query_ref.shape[1], kv_ref.shape[1] // 2
    for j in range(0, queries + 2 * keys, 128):
        part = total[:, j : j + 128]
        if j < queries + keys:
            part = rope_pair(part, cosine, sine)
        if j < queries:
            query_ref[:, j : j + 128] = part.astype(BF16)
        else:
            kv_ref[:, j - queries : j - queries + 128] = part.astype(BF16)


def project_gathered_kernel(slab, others, where_ref, left_ref, *refs):
    own, blocks, groups, (out_ref, whole_ref) = split_refs(refs, others, 2)
    assemble(where_ref, whole_ref, own, blocks, groups, others)
    for k in range(len(others) + 1):
        out_ref[:, slab_of(where_ref, k, slab)] = dot_nt(left_ref[...], whole_ref[k])


def project_out_kernel(slab, where_ref, left_ref, whole_ref, out_ref):
    for k in range(whole_ref.shape[0]):
        out_ref[:, slab_of(where_ref, k, slab)] = dot_nt(left_ref[...], whole_ref[k, :slab, :])


def project_back_kernel(slab, where_ref, left_ref, whole_ref, out_ref):
    total = None
    for k in range(whole_ref.shape[0]):
        part = dot_nn(left_ref[:, slab_of(where_ref, k, slab)], whole_ref[k, :slab, :])
        total = part if total is None else total + part
    out_ref[...] = total.astype(out_ref.dtype)


def allowed_pairs(ctx, positions):
    count = positions.shape[1]
    shape = (2 * count, count)
    key = lax.broadcasted_iota(jnp.int32, shape, 0)
    key = jnp.where(key < count, ctx * count + key, (1 - ctx) * count + key - count)
    query = ctx * count + lax.broadcasted_iota(jnp.int32, shape, 1)
    return (key <= query) & (key >= query - positions)


def attend_kernel(where_ref, positions_ref, query_ref, kv_ref, out_ref, lse_ref):
    keys = kv_ref.shape[1] // 2
    groups = keys // HEAD_DIM
    pairs = query_ref.shape[1] // 128 // groups
    allowed = allowed_pairs(where_ref[2], positions_ref[...])
    for g in range(groups):
        key = kv_ref[:, g * HEAD_DIM : (g + 1) * HEAD_DIM]
        value_t = kv_ref[:, keys + g * HEAD_DIM : keys + (g + 1) * HEAD_DIM].T

        def step(i, carry, g=g, key=key, value_t=value_t):
            at = g * pairs + i
            columns = pl.ds(pl.multiple_of(at * 128, 128), 128)
            query = query_ref[:, columns]
            attended, sums = [], []
            for h in range(2):
                scores = dot_nt(key, query[:, h * HEAD_DIM : (h + 1) * HEAD_DIM])
                scores = jnp.where(allowed, scores * HEAD_DIM ** (-0.5), NEG_FILL)
                largest = jnp.max(scores, axis=0, keepdims=True)
                exponent = jnp.exp(scores - largest)
                totals = jnp.sum(exponent, axis=0, keepdims=True)
                attended.append(dot_nn(value_t, (exponent / totals).astype(BF16)))
                sums.append(largest + jnp.log(totals))
            out_ref[:, columns] = jnp.concatenate(attended, axis=0).T.astype(BF16)
            lse_ref[at] = jnp.concatenate(sums, axis=0)
            return carry

        lax.fori_loop(0, pairs, step, 0)


def attend_back_kernel(
    where_ref,
    positions_ref,
    query_ref,
    kv_ref,
    lse_ref,
    grad_ref,
    cosine_ref,
    sine_ref,
    grad_query_ref,
    grad_kv_ref,
):
    keys = kv_ref.shape[1] // 2
    groups = keys // HEAD_DIM
    pairs = query_ref.shape[1] // 128 // groups
    scale = HEAD_DIM ** (-0.5)
    allowed = allowed_pairs(where_ref[2], positions_ref[...])
    cosine, sine = cosine_ref[...], sine_ref[...]
    grad_kv_ref[...] = jnp.zeros_like(grad_kv_ref)
    for g in range(groups):
        key_columns = slice(g * HEAD_DIM, (g + 1) * HEAD_DIM)
        value_columns = slice(keys + g * HEAD_DIM, keys + (g + 1) * HEAD_DIM)
        key, value = kv_ref[:, key_columns], kv_ref[:, value_columns]
        key_t = key.T

        def step(i, carry, g=g, key=key, value=value, key_t=key_t):
            at = g * pairs + i
            columns = pl.ds(pl.multiple_of(at * 128, 128), 128)
            query, grad, lse = query_ref[:, columns], grad_ref[:, columns], lse_ref[at]
            grad_query, grad_key, grad_value = [], 0.0, 0.0
            for h in range(2):
                head = slice(h * HEAD_DIM, (h + 1) * HEAD_DIM)
                scores = jnp.where(allowed, dot_nt(key, query[:, head]) * scale, NEG_FILL)
                probs = jnp.exp(scores - lse[h : h + 1])
                grad_probs = dot_nt(value, grad[:, head])
                row_dot = jnp.sum(probs * grad_probs, axis=0, keepdims=True)
                grad_scores = (probs * (grad_probs - row_dot)).astype(BF16)
                grad_query.append(dot_nn(key_t, grad_scores) * scale)
                grad_key += dot_nn(grad_scores, query[:, head])
                grad_value += dot_nn(probs.astype(BF16), grad[:, head])
            turned = jnp.concatenate(grad_query, axis=0).T
            grad_query_ref[:, columns] = unrope_pair(turned, cosine, sine).astype(BF16)
            return carry[0] + grad_key, carry[1] + grad_value

        zero = jnp.zeros((kv_ref.shape[0], HEAD_DIM), F32)
        grad_key, grad_value = lax.fori_loop(0, pairs, step, (zero, zero))
        grad_kv_ref[:, key_columns] = grad_key * scale
        grad_kv_ref[:, value_columns] = grad_value


def finish_kv_kernel(where_ref, grad_query_ref, mine_ref, other_ref, cosine_ref, sine_ref, out_ref):
    queries, keys = grad_query_ref.shape[1], mine_ref.shape[1] // 2
    out_ref[:, :queries] = grad_query_ref[...]
    total = mine_ref[...] + other_ref[...]
    for j in range(0, keys, 128):
        turned = unrope_pair(total[:, j : j + 128], cosine_ref[...], sine_ref[...])
        out_ref[:, queries + j : queries + j + 128] = turned.astype(BF16)
    out_ref[:, queries + keys :] = total[:, keys:].astype(BF16)


def hidden_kernel(hidden, slab, where_ref, *refs):
    gate_up_ref, down_ref = refs[-2:]
    far = (len(refs) - 2) // 2
    padded, half = down_ref.shape[0], hidden // 2
    places = ((gate_up_ref, 0), (gate_up_ref, padded), (down_ref, 0))
    for i, (out_ref, base) in enumerate(places):
        for k in range(far):
            for r in range(2):
                columns = slab_of(where_ref, 2 * k + r, slab)
                out_ref[base : base + half, columns] = refs[k][r, i]
                out_ref[base + half : base + hidden, columns] = refs[far + k][r, i]
        if padded > hidden:
            out_ref[base + hidden : base + padded, :] = jnp.zeros(
                (padded - hidden, out_ref.shape[1]), out_ref.dtype
            )


def feed_kernel(where_ref, normed_ref, rows_ref, grad_act_ref, grads_ref, act_ref):
    padded = act_ref.shape[1]
    for t in range(0, normed_ref.shape[0], 256):
        lin = dot_nt(normed_ref[t : t + 256, :], rows_ref[...])
        gate, up, grad_act = lin[:, :padded], lin[:, padded:], grad_act_ref[t : t + 256, :]
        below = 1.0 + jnp.exp(-gate)
        sigmoid, silu = 1.0 / below, gate / below
        act_ref[t : t + 256, :] = (silu * up).astype(BF16)
        grad_gate = grad_act * up * sigmoid * (1.0 + gate * (1.0 - sigmoid))
        grads_ref[t : t + 256, :padded] = grad_gate.astype(BF16)
        grads_ref[t : t + 256, padded:] = (grad_act * silu).astype(BF16)


def outer_kernel(half, where_ref, mine_ref, other_ref, *refs):
    blocks, out_ref = refs[:-1], refs[-1]
    here = pl.ds(pl.multiple_of(where_ref[1] * half, 16), half)
    there = pl.ds(pl.multiple_of((1 - where_ref[1]) * half, 16), half)
    total = None
    for k, block in enumerate(blocks):
        part = dot_tn(mine_ref[k], block[here, :]) + dot_tn(other_ref[k], block[there, :])
        total = part if total is None else total + part
    out_ref[...] = total


def owned(got, other, where):
    far = len(got)
    _, count, half_hidden, slab = got[0].shape
    total = far * 4 * half_hidden
    return local_kernel(
        functools.partial(owned_kernel, far, count, half_hidden),
        [jax.ShapeDtypeStruct((slab, total), F32)] * count,
        [pltpu.VMEM((total, slab), F32)],
        where,
        *got,
        *other,
    )


def layer(
    plane,
    tokens_in,
    doc_positions,
    attn_gain,
    query_weight,
    key_weight,
    value_weight,
    output_weight,
    mlp_gain,
    gate_weight,
    up_weight,
    down_weight,
    cotangent,
):
    nf = plane.size
    me = lax.axis_index("fsdp")
    high, low = me // 2, me % 2
    ctx = lax.axis_index("ctx")
    core = lax.axis_index("tp")
    rows, width = tokens_in.shape
    half_rows = rows // 2
    slab = query_weight.shape[0]
    query_columns = query_weight.shape[1]
    key_columns = key_weight.shape[1]
    hidden = gate_weight.shape[1] // nf
    half_hidden = hidden // 2

    def my_half(array):
        return lax.dynamic_slice_in_dim(array, core * half_rows, half_rows, 0)

    def tp_order(mine, other):
        here = core == 0
        return jnp.where(here, mine, other), jnp.where(here, other, mine)

    def tp_sum(partial):
        return partial + plane.swap_tp(partial)

    def plane_rows(array):
        mine = jnp.concatenate(plane.gather(my_half(array)), axis=0)
        return mine, plane.swap_tp(mine)

    def columns_near(array):
        mine, parity = lax.optimization_barrier((my_half(array), low))
        blocks = [mine[:, i * slab : (i + 1) * slab] for i in range(nf)]
        return plane.exchange_near(blocks, parity)

    fences = Fences(doc_positions[0])

    gain_rows = jnp.zeros((16, query_columns + 2 * key_columns), BF16)
    gain_rows = gain_rows.at[0, :slab].set(attn_gain).at[1, :slab].set(mlp_gain)
    qkv_shard = jnp.concatenate(
        [jnp.concatenate([query_weight, key_weight, value_weight], axis=1), gain_rows], axis=0
    )
    shared_rows = slab * 5 // 16 // 16 * 16
    qkv_own, qkv_blocks, qkv_groups, qkv_others = plane.gather_shared(qkv_shard, ctx, shared_rows)
    wo_own, wo_blocks, wo_groups, wo_others = plane.gather_shared(output_weight, ctx, shared_rows)
    cot_all = plane_rows(cotangent)

    mlp_shard = jnp.stack([gate_weight.T, up_weight.T, down_weight.T])
    mlp_halves = mlp_shard.reshape(3, nf, 2, half_hidden, slab)
    mlp_sent = jnp.where(ctx == 0, mlp_halves[:, :, 0], mlp_halves[:, :, 1])
    mlp_kept, mlp_got = plane.exchange_near([mlp_sent[:, i] for i in range(nf)], low)
    mlp_blocks = plane.exchange_far(mlp_kept, mlp_got, high)

    fences.cut()
    fences.cut()
    fences.cut()
    fences.cut()
    fences.cut()
    tokens = tokens_in.astype(F32)
    rms_one = lax.rsqrt(jnp.mean(tokens * tokens, axis=-1, keepdims=True) + EPSILON)
    scaled_one = tokens * rms_one
    where = jnp.stack([me, core, ctx]).astype(jnp.int32)
    cosine, sine = pair_tables(doc_positions)
    queries, kv_mine, normed_one, gains, qkv_whole = local_kernel(
        functools.partial(project_in_kernel, slab, qkv_others),
        [
            jax.ShapeDtypeStruct((rows, query_columns), BF16),
            jax.ShapeDtypeStruct((rows, 2 * key_columns), BF16),
            jax.ShapeDtypeStruct((rows, width), BF16),
            jax.ShapeDtypeStruct((16, width), F32),
            jax.ShapeDtypeStruct((nf,) + qkv_shard.shape, BF16),
        ],
        [],
        where,
        tokens_in,
        cosine,
        sine,
        qkv_own,
        *qkv_blocks,
        *qkv_groups,
    )
    gain_one, gain_two = gains[0:1], gains[1:2]

    def outer(got, blocks):
        mine = jnp.concatenate(got)
        return local_kernel(
            functools.partial(outer_kernel, half_rows),
            [jax.ShapeDtypeStruct((slab, blocks[0].shape[1]), F32)],
            [],
            where,
            mine,
            plane.swap_tp(mine),
            *blocks,
        )[0]

    kv_other = plane.swap_ctx(kv_mine)
    kv_mine, queries = fences.cut(kv_mine, queries)
    kv_all = jnp.concatenate([kv_mine, kv_other], axis=0)
    positions = doc_positions[None, :]
    attended_low, lse = local_kernel(
        attend_kernel,
        [
            jax.ShapeDtypeStruct((rows, query_columns), BF16),
            jax.ShapeDtypeStruct((query_columns // 128, 2, rows), F32),
        ],
        [],
        where,
        positions,
        queries,
        kv_all,
    )
    attended_low = fences.cut(attended_low)
    branch, wo_whole = local_kernel(
        functools.partial(project_gathered_kernel, slab, wo_others),
        [
            jax.ShapeDtypeStruct((rows, width), F32),
            jax.ShapeDtypeStruct((nf,) + output_weight.shape, BF16),
        ],
        [],
        where,
        attended_low,
        wo_own,
        *wo_blocks,
        *wo_groups,
    )
    residual = tokens + tp_sum(branch)
    rms_two = lax.rsqrt(jnp.mean(residual * residual, axis=-1, keepdims=True) + EPSILON)
    scaled_two = residual * rms_two
    normed_two = (scaled_two * gain_two).astype(BF16)

    normed_all = plane_rows(normed_two)
    fences.cut()
    fences.cut()
    fences.cut()
    fences.cut()
    padded = -(-hidden // 128) * 128
    gate_up_t, down_t = local_kernel(
        functools.partial(hidden_kernel, hidden, slab),
        [
            jax.ShapeDtypeStruct((2 * padded, width), BF16),
            jax.ShapeDtypeStruct((padded, width), BF16),
        ],
        [],
        where,
        *mlp_blocks,
        *(plane.swap_ctx(b) for b in mlp_blocks),
    )
    attended_all = plane.gather(attended_low)
    normed_near = columns_near(fences.after(normed_one))
    normed_got = plane.exchange_far(*normed_near, high)
    grads, acts = [], []
    for h in range(2):
        grad_h, act_h = local_kernel(
            feed_kernel,
            [
                jax.ShapeDtypeStruct((nf * half_rows, 2 * padded), BF16),
                jax.ShapeDtypeStruct((nf * half_rows, padded), BF16),
            ],
            [],
            where,
            normed_all[h],
            gate_up_t,
            dot_nt(cot_all[h], down_t),
        )
        grads.append(grad_h)
        acts.append(act_h)

    def ctx_half(whole, first):
        middle, last = first + half_hidden, first + hidden
        got = plane.swap_ctx(fences.after(whole[middle:last]))
        return sum(lax.optimization_barrier((whole[first:middle], got)))

    def owners_near(halves):
        blocks = [
            jnp.stack([h[:, i * slab : (i + 1) * slab] for h in halves]) for i in range(nf)
        ]
        return plane.exchange_near(blocks, low)

    def from_owners(got):
        other = [plane.swap_ctx(g) for g in got]
        where = jnp.stack([high, low, ctx]).astype(jnp.int32)
        return owned(got, other, where)

    def tp_part(lefts, right, wire):
        other = plane.swap_tp(dot_nn(lefts[1], right).astype(wire)).astype(F32)
        mine = dot_nn(lefts[0], right) + other
        return plane.reduce_near(mine.reshape(nf, half_rows, -1), wire)

    def whole_rows(mine):
        one, two = tp_order(mine, plane.swap_tp(mine))
        return jnp.concatenate([one, two], axis=0)

    pieces = 4
    step = width // pieces
    near = []
    reduced = []

    def piece(i):
        lefts = [fences.after(g) for g in grads]
        near.append(tp_part(lefts, gate_up_t[:, i * step : (i + 1) * step], F32))

    def piece_far(i):
        reduced.append(plane.reduce_far(near[i][0] + near[i][1]))

    grads[0], grads[1], acts[0], acts[1] = fences.cut(*grads, *acts)
    piece(0)
    piece(1)
    half_down = ctx_half(sum(dot_tn(fences.after(a), c) for a, c in zip(acts, cot_all)), 0)
    fences.cut()
    piece_far(0)
    piece(2)
    gate_up_grad = sum(dot_tn(fences.after(g), n) for g, n in zip(grads, normed_all))
    half_gate = ctx_half(gate_up_grad, 0)
    fences.cut()
    piece_far(1)
    piece(3)
    half_up = ctx_half(gate_up_grad, padded)
    fences.cut()
    piece_far(2)
    mlp_kept, mlp_odd = tp_part([fences.after(a) for a in acts], down_t, BF16)
    down_near = owners_near([half_down])
    fences.cut()
    piece_far(3)
    gate_up_near = owners_near([half_gate, half_up])
    fences.cut()
    down_got = plane.exchange_far(*down_near, high)
    fences.cut()
    grad_normed_two = whole_rows(jnp.concatenate(reduced, axis=-1))
    fences.cut()
    grad_out = cotangent.astype(F32)
    scaled_grad_two = grad_normed_two * gain_two
    grad_residual = (
        grad_out
        + rms_two * scaled_grad_two
        - residual
        * (rms_two * rms_two * rms_two)
        * jnp.mean(scaled_grad_two * residual, axis=-1, keepdims=True)
    )
    grad_attn_low = grad_residual.astype(BF16)
    grad_attended = local_kernel(
        functools.partial(project_back_kernel, slab),
        [jax.ShapeDtypeStruct((rows, query_columns), BF16)],
        [],
        where,
        grad_attn_low,
        wo_whole,
    )[0]
    grad_attn_near = columns_near(fences.after(grad_attn_low))
    grad_attended = fences.cut(grad_attended)
    grad_query, kv_grads = local_kernel(
        attend_back_kernel,
        [
            jax.ShapeDtypeStruct((rows, query_columns), BF16),
            jax.ShapeDtypeStruct((2 * rows, 2 * key_columns), F32),
        ],
        [],
        where,
        positions,
        queries,
        kv_all,
        lse,
        grad_attended,
        cosine,
        sine,
    )
    kv_grads, grad_query = fences.cut(kv_grads, grad_query)
    mlp_mine = plane.reduce_far(mlp_kept + mlp_odd.astype(F32), BF16)
    grad_attn_got = plane.exchange_far(*grad_attn_near, high)
    (grad_qkv_lin,) = local_kernel(
        finish_kv_kernel,
        [jax.ShapeDtypeStruct((rows, query_columns + 2 * key_columns), BF16)],
        [],
        where,
        grad_query,
        kv_grads[:rows],
        plane.swap_ctx(kv_grads[rows:]),
        cosine,
        sine,
    )
    grad_qkv_all = plane.gather(grad_qkv_lin)
    fences.cut()
    gate_up_got = plane.exchange_far(*gate_up_near, high)
    grad_normed_one = tp_sum(
        local_kernel(
            functools.partial(project_out_kernel, slab),
            [jax.ShapeDtypeStruct((rows, width), F32)],
            [],
            where,
            fences.after(grad_qkv_lin),
            qkv_whole,
        )[0],
    )
    fences.cut()
    gain_sums = plane.sum_all(
        jnp.stack(
            [
                jnp.sum(grad_normed_one * scaled_one, axis=0),
                jnp.sum(grad_normed_two * scaled_two, axis=0),
            ]
        ),
    )
    fences.cut()
    grad_wo = outer(grad_attn_got, [fences.after(b) for b in attended_all])
    fences.cut()
    grad_qkv = outer(normed_got, [fences.after(b) for b in grad_qkv_all])
    fences.cut()
    fences.cut()
    fences.cut()
    scaled_grad_one = grad_normed_one * gain_one
    grad_tokens = (
        grad_residual
        + rms_one * scaled_grad_one
        - tokens
        * (rms_one * rms_one * rms_one)
        * jnp.mean(scaled_grad_one * tokens, axis=-1, keepdims=True)
    )

    output_grad = grad_wo + plane.swap_ctx(grad_wo)
    block_out = (fences.after(residual) + whole_rows(mlp_mine)).astype(BF16)
    grad_qkv = grad_qkv + plane.swap_ctx(grad_qkv)
    query_grad = grad_qkv[:, :query_columns]
    key_grad = grad_qkv[:, query_columns : query_columns + key_columns]
    value_grad = grad_qkv[:, query_columns + key_columns :]
    (down_grad,) = from_owners(down_got)
    gate_grad, up_grad = from_owners(gate_up_got)

    gain_sums = lax.dynamic_slice_in_dim(gain_sums, me * slab, slab, 1)
    gain_sums = jnp.where(fences.value > 0, gain_sums, 0.0)
    return (
        block_out,
        grad_tokens,
        gain_sums[0],
        query_grad,
        key_grad,
        value_grad,
        output_grad,
        gain_sums[1],
        gate_grad,
        up_grad,
        down_grad,
    )


def rotary_tables(positions):
    half_dim = HEAD_DIM // 2
    inverse = 1.0 / 10000.0 ** (jnp.arange(half_dim, dtype=F32) * (2.0 / HEAD_DIM))
    angles = positions.astype(F32)[:, None] * inverse[None, :]
    cosine_table = jnp.concatenate([jnp.cos(angles), jnp.cos(angles)], axis=-1)[:, None, :]
    sine_table = jnp.concatenate([jnp.sin(angles), jnp.sin(angles)], axis=-1)[:, None, :]
    return (cosine_table, sine_table)


def apply_rotary(values, cosine_table, sine_table):
    half_dim = values.shape[-1] // 2
    turned = jnp.concatenate([-values[..., half_dim:], values[..., :half_dim]], axis=-1)
    return values * cosine_table + turned * sine_table


def undo_rotary(gradient, cosine_table, sine_table):
    half_dim = gradient.shape[-1] // 2
    sined = gradient * sine_table
    return gradient * cosine_table + jnp.concatenate(
        [sined[..., half_dim:], -sined[..., :half_dim]], axis=-1
    )


def contract_last(left_array, right_array):
    return lax.dot_general(
        left_array, right_array, (((1,), (1,)), ((), ())), preferred_element_type=F32
    )


def contract_first(left_array, right_array):
    return lax.dot_general(
        left_array, right_array, (((0,), (0,)), ((), ())), preferred_element_type=F32
    )


def normed_fold(scaled, pieces):
    gain_float = pieces[0].astype(F32)
    normed = (scaled * gain_float[None, :]).astype(BF16)
    sums = tuple(
        (jnp.dot(normed, matrix, preferred_element_type=F32) for matrix in pieces[1:])
    )
    return sums + (normed, gain_float)


def row_fold(left_array, shard_piece):
    return jnp.dot(left_array, shard_piece, preferred_element_type=F32)


def column_fold(gradients_in, pieces):
    part_sum = contract_last(gradients_in[0], pieces[0])
    for grad_piece, weight_piece in zip(gradients_in[1:], pieces[1:]):
        part_sum = part_sum + contract_last(grad_piece, weight_piece)
    return part_sum


def column_map(left_array, shard_piece):
    return contract_last(left_array, shard_piece)


def tensor_total(partial_sum):
    return lax.psum(partial_sum, "tp")


def rows_body(
    tokens_in,
    doc_positions,
    attn_gain,
    query_weight,
    key_weight,
    value_weight,
    output_weight,
    mlp_gain,
    gate_weight,
    up_weight,
    down_weight,
    cotangent,
):
    local_rows = tokens_in.shape[0]
    query_columns = query_weight.shape[1]
    key_columns = key_weight.shape[1]
    local_groups = key_columns // HEAD_DIM
    group_size = HEADS // KV_HEADS
    group_width = group_size * HEAD_DIM
    score_scale = HEAD_DIM ** (-0.5)
    tokens = tokens_in.astype(F32)
    rms_one = lax.rsqrt(jnp.mean(tokens * tokens, axis=-1, keepdims=True) + EPSILON)
    scaled_one = tokens * rms_one
    query_lin, key_lin, value_lin, normed_one, gain_one = normed_fold(
        scaled_one,
        (
            lax.all_gather(attn_gain, "fsdp", axis=0, tiled=True),
            lax.all_gather(query_weight, "fsdp", axis=0, tiled=True),
            lax.all_gather(key_weight, "fsdp", axis=0, tiled=True),
            lax.all_gather(value_weight, "fsdp", axis=0, tiled=True),
        ),
    )
    cosine_table, sine_table = rotary_tables(doc_positions)
    queries = (
        apply_rotary(query_lin.reshape(local_rows, -1, HEAD_DIM), cosine_table, sine_table)
        .astype(BF16)
        .reshape(local_rows, query_columns)
    )
    keys_low = (
        apply_rotary(key_lin.reshape(local_rows, -1, HEAD_DIM), cosine_table, sine_table)
        .astype(BF16)
        .reshape(local_rows, key_columns)
    )
    values_low = value_lin.astype(BF16)
    key_all, value_all = (
        lax.all_gather(keys_low, "ctx", axis=0, tiled=True),
        lax.all_gather(values_low, "ctx", axis=0, tiled=True),
    )
    key_count = key_all.shape[0]
    query_places = lax.axis_index("ctx") * local_rows + jnp.arange(local_rows, dtype=jnp.int32)
    key_places = jnp.arange(key_count, dtype=jnp.int32)
    allowed = (key_places[None, :] <= query_places[:, None]) & (
        key_places[None, :] >= (query_places - doc_positions)[:, None]
    )

    def head_scores(query_group, key_head):
        raw_scores = (
            jnp.einsum("ngd,kd->gnk", query_group, key_head, preferred_element_type=F32)
            * score_scale
        )
        return jnp.where(allowed[None], raw_scores, NEG_FILL)

    attended_parts = []
    lse_parts = []
    for group_index in range(local_groups):
        query_group = queries[
            :, group_index * group_width : (group_index + 1) * group_width
        ].reshape(local_rows, group_size, HEAD_DIM)
        key_head = key_all[:, group_index * HEAD_DIM : (group_index + 1) * HEAD_DIM]
        value_head = value_all[:, group_index * HEAD_DIM : (group_index + 1) * HEAD_DIM]
        scores = head_scores(query_group, key_head)
        largest = jnp.max(scores, axis=-1, keepdims=True)
        exponent = jnp.exp(scores - largest)
        totals = jnp.sum(exponent, axis=-1, keepdims=True)
        probs_low = (exponent / totals).astype(BF16)
        attended_parts.append(
            jnp.einsum(
                "gnk,kd->ngd", probs_low, value_head, preferred_element_type=F32
            ).reshape(local_rows, group_width)
        )
        lse_parts.append(largest + jnp.log(totals))
    attended_low = jnp.concatenate(attended_parts, axis=1).astype(BF16)
    attn_branch = tensor_total(
        column_map(attended_low, lax.all_gather(output_weight, "fsdp", axis=0, tiled=True))
    )
    residual = tokens + attn_branch
    rms_two = lax.rsqrt(jnp.mean(residual * residual, axis=-1, keepdims=True) + EPSILON)
    scaled_two = residual * rms_two
    gate_lin, up_lin, normed_two, gain_two = normed_fold(
        scaled_two,
        (
            lax.all_gather(mlp_gain, "fsdp", axis=0, tiled=True),
            lax.all_gather(gate_weight, "fsdp", axis=0, tiled=True),
            lax.all_gather(up_weight, "fsdp", axis=0, tiled=True),
        ),
    )
    silu_value = gate_lin / (1.0 + jnp.exp(-gate_lin))
    act_low = (silu_value * up_lin).astype(BF16)
    mlp_branch = tensor_total(
        column_map(act_low, lax.all_gather(down_weight, "fsdp", axis=0, tiled=True))
    )
    block_out = (residual + mlp_branch).astype(BF16)
    grad_out = cotangent.astype(F32)
    grad_act = row_fold(cotangent, lax.all_gather(down_weight, "fsdp", axis=0, tiled=True))
    sigmoid = 1.0 / (1.0 + jnp.exp(-gate_lin))
    grad_gate_lin = (grad_act * up_lin * sigmoid * (1.0 + gate_lin * (1.0 - sigmoid))).astype(
        BF16
    )
    grad_up_lin = (grad_act * silu_value).astype(BF16)
    grad_normed_two = tensor_total(
        column_fold(
            (grad_gate_lin, grad_up_lin),
            (
                lax.all_gather(gate_weight, "fsdp", axis=0, tiled=True),
                lax.all_gather(up_weight, "fsdp", axis=0, tiled=True),
            ),
        )
    )
    scaled_grad_two = grad_normed_two * gain_two[None, :]
    grad_residual = (
        grad_out
        + rms_two * scaled_grad_two
        - residual
        * (rms_two * rms_two * rms_two)
        * jnp.mean(scaled_grad_two * residual, axis=-1, keepdims=True)
    )
    grad_attn_low = grad_residual.astype(BF16)
    grad_attended = row_fold(
        grad_attn_low, lax.all_gather(output_weight, "fsdp", axis=0, tiled=True)
    ).astype(BF16)
    query_grads = []
    key_grads = []
    value_grads = []
    for group_index in range(local_groups):
        query_group = queries[
            :, group_index * group_width : (group_index + 1) * group_width
        ].reshape(local_rows, group_size, HEAD_DIM)
        key_head = key_all[:, group_index * HEAD_DIM : (group_index + 1) * HEAD_DIM]
        value_head = value_all[:, group_index * HEAD_DIM : (group_index + 1) * HEAD_DIM]
        probabilities = jnp.exp(head_scores(query_group, key_head) - lse_parts[group_index])
        probs_low = probabilities.astype(BF16)
        grad_group = grad_attended[
            :, group_index * group_width : (group_index + 1) * group_width
        ].reshape(local_rows, group_size, HEAD_DIM)
        grad_probs = jnp.einsum(
            "ngd,kd->gnk", grad_group, value_head, preferred_element_type=F32
        )
        row_dot = jnp.sum(probabilities * grad_probs, axis=-1, keepdims=True)
        grad_scores = (probabilities * (grad_probs - row_dot)).astype(BF16)
        query_grads.append(
            jnp.einsum("gnk,kd->ngd", grad_scores, key_head, preferred_element_type=F32)
            * score_scale
        )
        key_grads.append(
            jnp.einsum("gnk,ngd->kd", grad_scores, query_group, preferred_element_type=F32)
            * score_scale
        )
        value_grads.append(
            jnp.einsum("gnk,ngd->kd", probs_low, grad_group, preferred_element_type=F32)
        )
    key_grad_local, value_grad_local = (
        lax.psum_scatter(
            jnp.concatenate(key_grads, axis=1), "ctx", scatter_dimension=0, tiled=True
        ),
        lax.psum_scatter(
            jnp.concatenate(value_grads, axis=1), "ctx", scatter_dimension=0, tiled=True
        ),
    )
    grad_q_lin = (
        undo_rotary(jnp.concatenate(query_grads, axis=1), cosine_table, sine_table)
        .astype(BF16)
        .reshape(local_rows, query_columns)
    )
    grad_k_lin = (
        undo_rotary(key_grad_local.reshape(local_rows, -1, HEAD_DIM), cosine_table, sine_table)
        .astype(BF16)
        .reshape(local_rows, key_columns)
    )
    grad_v_lin = value_grad_local.astype(BF16)
    grad_normed_one = tensor_total(
        column_fold(
            (grad_q_lin, grad_k_lin, grad_v_lin),
            (
                lax.all_gather(query_weight, "fsdp", axis=0, tiled=True),
                lax.all_gather(key_weight, "fsdp", axis=0, tiled=True),
                lax.all_gather(value_weight, "fsdp", axis=0, tiled=True),
            ),
        )
    )
    scaled_grad_one = grad_normed_one * gain_one[None, :]
    grad_tokens = (
        grad_residual
        + rms_one * scaled_grad_one
        - tokens
        * (rms_one * rms_one * rms_one)
        * jnp.mean(scaled_grad_one * tokens, axis=-1, keepdims=True)
    )
    owned = lax.psum_scatter(
        (
            jnp.sum(grad_normed_one * scaled_one, axis=0),
            contract_first(normed_one, grad_q_lin),
            contract_first(normed_one, grad_k_lin),
            contract_first(normed_one, grad_v_lin),
            contract_first(grad_attn_low, attended_low),
            jnp.sum(grad_normed_two * scaled_two, axis=0),
            contract_first(normed_two, grad_gate_lin),
            contract_first(normed_two, grad_up_lin),
            contract_first(cotangent, act_low),
        ),
        "fsdp",
        scatter_dimension=0,
        tiled=True,
    )
    (
        gain_one_grad,
        query_grad,
        key_grad,
        value_grad,
        output_grad,
        gain_two_grad,
        gate_grad,
        up_grad,
        down_grad,
    ) = owned
    summed = lax.psum(
        (
            gain_one_grad,
            query_grad,
            key_grad,
            value_grad,
            output_grad,
            gain_two_grad,
            gate_grad,
            up_grad,
            down_grad,
        ),
        "ctx",
    )
    return (
        block_out,
        grad_tokens,
        summed[0],
        summed[1],
        summed[2],
        summed[3],
        summed[4],
        summed[5],
        summed[6],
        summed[7],
        summed[8],
    )


def choose_body(size, *arrays):
    rows, width = arrays[0].shape
    if size * rows <= width:
        return layer(Plane(size), *arrays)
    return rows_body(*arrays)


def solution(mesh):
    rows = P(("fsdp", "ctx"), None)
    weight = P("fsdp", "tp")
    gain = P("fsdp")
    return jax.shard_map(
        functools.partial(choose_body, mesh.shape["fsdp"]),
        mesh=mesh,
        in_specs=(
            rows,
            P(("fsdp", "ctx")),
            gain,
            weight,
            weight,
            weight,
            weight,
            gain,
            weight,
            weight,
            weight,
            rows,
        ),
        out_specs=(rows, rows, gain, weight, weight, weight, weight, gain, weight, weight, weight),
        check_vma=False,
    )
```

```python
import functools

import jax
import jax.numpy as jnp
from jax import lax
from jax.experimental import pallas as pl
from jax.experimental.pallas import tpu as pltpu
from jax.sharding import PartitionSpec as P


HEADS = 32
KV_HEADS = 4
HEAD_DIM = 64

EPSILON = 1e-05
NEG_FILL = -1e30


F32 = jnp.float32
BF16 = jnp.bfloat16


def pair_tables(positions):
    half_dim = HEAD_DIM // 2
    inverse = 1.0 / 10000.0 ** (jnp.arange(half_dim, dtype=F32) * (2.0 / HEAD_DIM))
    angles = positions.astype(F32)[:, None] * inverse[None, :]
    return jnp.tile(jnp.cos(angles), (1, 4)), jnp.tile(jnp.sin(angles), (1, 4))


def first_half(shape):
    return lax.broadcasted_iota(jnp.int32, shape, 1) % HEAD_DIM < HEAD_DIM // 2


def rope_pair(values, cosine, sine):
    span, half_dim = values.shape[1], HEAD_DIM // 2
    ahead, behind = pltpu.roll(values, span - half_dim, 1), pltpu.roll(values, half_dim, 1)
    return values * cosine + jnp.where(first_half(values.shape), -ahead, behind) * sine


def unrope_pair(gradient, cosine, sine):
    span, half_dim = gradient.shape[1], HEAD_DIM // 2
    sined = gradient * sine
    ahead, behind = pltpu.roll(sined, span - half_dim, 1), pltpu.roll(sined, half_dim, 1)
    return gradient * cosine + jnp.where(first_half(sined.shape), ahead, -behind)


def dot_nt(left, right):
    return lax.dot_general(left, right, (((1,), (1,)), ((), ())), preferred_element_type=F32)


def dot_tn(left, right):
    return lax.dot_general(left, right, (((0,), (0,)), ((), ())), preferred_element_type=F32)


def dot_nn(left, right):
    return jnp.dot(left, right, preferred_element_type=F32)


class Plane:
    def __init__(self, size):
        self.size = size
        self.far = size // 2

    def send(self, array, axis, pairs):
        return lax.ppermute(array, axis, pairs)

    def swap(self, array, step):
        pairs = [(i, i ^ step) for i in range(self.size)]
        return self.send(array, "fsdp", pairs)

    def swap_ctx(self, array):
        return self.send(array, "ctx", [(0, 1), (1, 0)])

    def swap_tp(self, array):
        return self.send(array, "tp", [(0, 1), (1, 0)])

    def sum_all(self, array):
        array = array + self.swap(array, 1)
        array = array + self.swap_ctx(array)
        return sum((self.swap(array, 2 * k) for k in range(1, self.far)), array)

    def gather_far(self, shard):
        far = [self.swap(shard, 2 * k) for k in range(1, self.far)]
        return [shard] + far

    def gather_near(self, blocks):
        out = []
        for block in blocks:
            out += [block, self.swap(block, 1)]
        return out

    def gather(self, shard):
        return self.gather_near(self.gather_far(shard))

    def gather_shared(self, shard, ctx, rows):
        first = shard.shape[0] - 2 * rows
        mine = jnp.where(ctx == 0, shard[first : first + rows], shard[first + rows :])
        blocks = self.gather(jnp.concatenate([shard[:first], mine]))
        groups = [(1, 2), (3, 4, 6), (5, 7)] if self.size == 8 else [range(1, self.size)]
        others = [None] * self.size
        for g, members in enumerate(groups):
            sent = jnp.stack([blocks[k][first:] for k in members])
            got = self.swap_ctx(sent)
            for j, k in enumerate(members):
                others[k] = (g, j)
            groups[g] = got
        return shard, blocks[1:], groups, others[1:]

    def exchange_near(self, blocks, low):
        here = low == 0
        kept = jnp.stack([jnp.where(here, a, b) for a, b in zip(blocks[0::2], blocks[1::2])])
        sent = jnp.stack([jnp.where(here, b, a) for a, b in zip(blocks[0::2], blocks[1::2])])
        return kept, self.swap(sent, 1)

    def exchange_far(self, kept, got, high):
        kept, high = lax.optimization_barrier((kept, high))
        out = []
        for k in range(self.far):
            block = jnp.stack(
                [lax.dynamic_index_in_dim(b, high ^ k, 0, keepdims=False) for b in (kept, got)]
            )
            out.append(self.swap(block, 2 * k) if k else block)
        return out

    def reduce_near(self, chunk, wire=F32):
        chunk = chunk.reshape(self.far, 2, *chunk.shape[1:])
        sent = chunk[:, 1].astype(wire)
        return chunk[:, 0].astype(F32), self.swap(sent, 1)

    def reduce_far(self, sums, wire=F32):
        got = [self.swap(sums[k].astype(wire), 2 * k) for k in range(1, self.far)]
        return sum((g.astype(F32) for g in got), sums[0])


class Fences:
    def __init__(self, seed):
        self.value = seed

    def cut(self, *before):
        value, *before = lax.optimization_barrier((self.value, *before))
        self.value = value + 1
        return before[0] if len(before) == 1 else before

    def after(self, array):
        array, self.value = lax.optimization_barrier((array, self.value))
        return array


def owned_kernel(far, count, half_hidden, place_ref, *refs):
    got, other = refs[:far], refs[far : 2 * far]
    outs, rows = refs[2 * far : 2 * far + count], refs[-1]
    me, ctx = place_ref[0], place_ref[2]
    for i in range(count):
        for k in range(far):
            for r in range(2):
                owner = me ^ (2 * k + r)
                first = pl.multiple_of((owner * 2 + ctx) * half_hidden, 8)
                second = pl.multiple_of((owner * 2 + 1 - ctx) * half_hidden, 8)
                rows[pl.ds(first, half_hidden), :] = got[k][r, i]
                rows[pl.ds(second, half_hidden), :] = other[k][r, i]
        for j in range(rows.shape[0] // 128):
            outs[i][:, j * 128 : (j + 1) * 128] = rows[j * 128 : (j + 1) * 128, :].T


WHOLE = pl.BlockSpec(memory_space=pltpu.VMEM)
SCALARS = pl.BlockSpec(memory_space=pltpu.SMEM)


def local_kernel(kernel, outs, scratch, *arrays):
    moved = sum(x.size * x.dtype.itemsize for x in (*arrays, *outs))
    return pl.pallas_call(
        kernel,
        out_shape=outs,
        in_specs=[SCALARS] + [WHOLE] * (len(arrays) - 1),
        out_specs=[WHOLE] * len(outs),
        scratch_shapes=scratch,
        compiler_params=pltpu.CompilerParams(vmem_limit_bytes=40 * 2**20),
        cost_estimate=pl.CostEstimate(flops=0, bytes_accessed=moved, transcendentals=0),
    )(*arrays)


def slab_of(where_ref, k, slab):
    return pl.ds(pl.multiple_of((where_ref[0] ^ k) * slab, 128), slab)


def assemble(where_ref, whole_ref, own, blocks, groups, others):
    rows = groups[0].shape[1]
    total = own.shape[0]
    first = total - 2 * rows
    here = pl.ds(pl.multiple_of(first + where_ref[2] * rows, 16), rows)
    there = pl.ds(pl.multiple_of(first + (1 - where_ref[2]) * rows, 16), rows)
    whole_ref[0] = own[...]
    for k, (block, (g, j)) in enumerate(zip(blocks, others)):
        whole_ref[k + 1, :first, :] = block[:first, :]
        whole_ref[k + 1, here, :] = block[first:, :]
        whole_ref[k + 1, there, :] = groups[g][j]


def split_refs(refs, others, outs):
    count = len(others)
    inputs = refs[: len(refs) - outs]
    return inputs[0], inputs[1 : 1 + count], inputs[1 + count :], refs[len(refs) - outs :]


def project_in_kernel(slab, others, where_ref, tokens_ref, cosine_ref, sine_ref, *refs):
    own, blocks, groups, outs = split_refs(refs, others, 5)
    query_ref, kv_ref, normed_ref, gains_ref, whole_ref = outs
    assemble(where_ref, whole_ref, own, blocks, groups, others)
    count = len(others) + 1
    for k in range(count):
        gains_ref[:, slab_of(where_ref, k, slab)] = whole_ref[k, slab:, :slab].astype(F32)
    tokens = tokens_ref[...].astype(F32)
    rms = lax.rsqrt(jnp.mean(tokens * tokens, axis=-1, keepdims=True) + EPSILON)
    normed_ref[...] = (tokens * rms * gains_ref[0:1, :]).astype(BF16)
    total = None
    for k in range(count):
        part = dot_nn(normed_ref[:, slab_of(where_ref, k, slab)], whole_ref[k, :slab, :])
        total = part if total is None else total + part
    cosine, sine = cosine_ref[...], sine_ref[...]
    queries, keys = query_ref.shape[1], kv_ref.shape[1] // 2
    for j in range(0, queries + 2 * keys, 128):
        part = total[:, j : j + 128]
        if j < queries + keys:
            part = rope_pair(part, cosine, sine)
        if j < queries:
            query_ref[:, j : j + 128] = part.astype(BF16)
        else:
            kv_ref[:, j - queries : j - queries + 128] = part.astype(BF16)


def project_gathered_kernel(slab, others, where_ref, left_ref, *refs):
    own, blocks, groups, (out_ref, whole_ref) = split_refs(refs, others, 2)
    assemble(where_ref, whole_ref, own, blocks, groups, others)
    for k in range(len(others) + 1):
        out_ref[:, slab_of(where_ref, k, slab)] = dot_nt(left_ref[...], whole_ref[k])


def project_out_kernel(slab, where_ref, left_ref, whole_ref, out_ref):
    for k in range(whole_ref.shape[0]):
        out_ref[:, slab_of(where_ref, k, slab)] = dot_nt(left_ref[...], whole_ref[k, :slab, :])


def project_back_kernel(slab, where_ref, left_ref, whole_ref, out_ref):
    total = None
    for k in range(whole_ref.shape[0]):
        part = dot_nn(left_ref[:, slab_of(where_ref, k, slab)], whole_ref[k, :slab, :])
        total = part if total is None else total + part
    out_ref[...] = total.astype(out_ref.dtype)


def allowed_pairs(ctx, positions):
    count = positions.shape[1]
    shape = (2 * count, count)
    key = lax.broadcasted_iota(jnp.int32, shape, 0)
    key = jnp.where(key < count, ctx * count + key, (1 - ctx) * count + key - count)
    query = ctx * count + lax.broadcasted_iota(jnp.int32, shape, 1)
    return (key <= query) & (key >= query - positions)


def attend_kernel(where_ref, positions_ref, query_ref, kv_ref, out_ref, lse_ref, key_ref, value_ref):
    groups = key_ref.shape[0]
    keys = groups * HEAD_DIM
    pairs = query_ref.shape[1] // 128 // groups
    allowed = allowed_pairs(where_ref[2], positions_ref[...])
    for g in range(groups):
        key_ref[g] = kv_ref[:, g * HEAD_DIM : (g + 1) * HEAD_DIM]
        value_ref[g] = kv_ref[:, keys + g * HEAD_DIM : keys + (g + 1) * HEAD_DIM].T

    def step(at, carry):
        g = lax.div(at, pairs)
        key, value_t = key_ref[g], value_ref[g]
        columns = pl.ds(pl.multiple_of(at * 128, 128), 128)
        query = query_ref[:, columns]
        attended, sums = [], []
        for h in range(2):
            scores = dot_nt(key, query[:, h * HEAD_DIM : (h + 1) * HEAD_DIM])
            scores = jnp.where(allowed, scores * HEAD_DIM ** (-0.5), NEG_FILL)
            largest = jnp.max(scores, axis=0, keepdims=True)
            exponent = jnp.exp(scores - largest)
            totals = jnp.sum(exponent, axis=0, keepdims=True)
            attended.append(dot_nn(value_t, (exponent / totals).astype(BF16)))
            sums.append(largest + jnp.log(totals))
        out_ref[:, columns] = jnp.concatenate(attended, axis=0).T.astype(BF16)
        lse_ref[at] = jnp.concatenate(sums, axis=0)
        return carry

    lax.fori_loop(0, groups * pairs, step, 0)


def attend_back_kernel(
    where_ref,
    positions_ref,
    query_ref,
    kv_ref,
    lse_ref,
    grad_ref,
    cosine_ref,
    sine_ref,
    grad_query_ref,
    grad_kv_ref,
):
    keys = kv_ref.shape[1] // 2
    groups = keys // HEAD_DIM
    pairs = query_ref.shape[1] // 128 // groups
    scale = HEAD_DIM ** (-0.5)
    allowed = allowed_pairs(where_ref[2], positions_ref[...])
    cosine, sine = cosine_ref[...], sine_ref[...]
    grad_kv_ref[...] = jnp.zeros_like(grad_kv_ref)
    for g in range(groups):
        key_columns = slice(g * HEAD_DIM, (g + 1) * HEAD_DIM)
        value_columns = slice(keys + g * HEAD_DIM, keys + (g + 1) * HEAD_DIM)
        key, value = kv_ref[:, key_columns], kv_ref[:, value_columns]
        key_t = key.T

        def step(i, carry, g=g, key=key, value=value, key_t=key_t):
            at = g * pairs + i
            columns = pl.ds(pl.multiple_of(at * 128, 128), 128)
            query, grad, lse = query_ref[:, columns], grad_ref[:, columns], lse_ref[at]
            grad_query, grad_key, grad_value = [], 0.0, 0.0
            for h in range(2):
                head = slice(h * HEAD_DIM, (h + 1) * HEAD_DIM)
                scores = jnp.where(allowed, dot_nt(key, query[:, head]) * scale, NEG_FILL)
                probs = jnp.exp(scores - lse[h : h + 1])
                grad_probs = dot_nt(value, grad[:, head])
                row_dot = jnp.sum(probs * grad_probs, axis=0, keepdims=True)
                grad_scores = (probs * (grad_probs - row_dot)).astype(BF16)
                grad_query.append(dot_nn(key_t, grad_scores) * scale)
                grad_key += dot_nn(grad_scores, query[:, head])
                grad_value += dot_nn(probs.astype(BF16), grad[:, head])
            turned = jnp.concatenate(grad_query, axis=0).T
            grad_query_ref[:, columns] = unrope_pair(turned, cosine, sine).astype(BF16)
            return carry[0] + grad_key, carry[1] + grad_value

        zero = jnp.zeros((kv_ref.shape[0], HEAD_DIM), F32)
        grad_key, grad_value = lax.fori_loop(0, pairs, step, (zero, zero))
        grad_kv_ref[:, key_columns] = grad_key * scale
        grad_kv_ref[:, value_columns] = grad_value


def finish_kv_kernel(where_ref, grad_query_ref, mine_ref, other_ref, cosine_ref, sine_ref, out_ref):
    queries, keys = grad_query_ref.shape[1], mine_ref.shape[1] // 2
    out_ref[:, :queries] = grad_query_ref[...]
    total = mine_ref[...] + other_ref[...]
    for j in range(0, keys, 128):
        turned = unrope_pair(total[:, j : j + 128], cosine_ref[...], sine_ref[...])
        out_ref[:, queries + j : queries + j + 128] = turned.astype(BF16)
    out_ref[:, queries + keys :] = total[:, keys:].astype(BF16)


def hidden_kernel(hidden, slab, where_ref, *refs):
    gate_up_ref, down_ref = refs[-2:]
    far = (len(refs) - 2) // 2
    padded, half = down_ref.shape[0], hidden // 2
    places = ((gate_up_ref, 0), (gate_up_ref, padded), (down_ref, 0))
    for i, (out_ref, base) in enumerate(places):
        for k in range(far):
            for r in range(2):
                columns = slab_of(where_ref, 2 * k + r, slab)
                out_ref[base : base + half, columns] = refs[k][r, i]
                out_ref[base + half : base + hidden, columns] = refs[far + k][r, i]
        if padded > hidden:
            out_ref[base + hidden : base + padded, :] = jnp.zeros(
                (padded - hidden, out_ref.shape[1]), out_ref.dtype
            )


def feed_kernel(where_ref, normed_ref, rows_ref, grad_act_ref, grads_ref, act_ref):
    padded = act_ref.shape[1]
    for t in range(0, normed_ref.shape[0], 256):
        lin = dot_nt(normed_ref[t : t + 256, :], rows_ref[...])
        gate, up, grad_act = lin[:, :padded], lin[:, padded:], grad_act_ref[t : t + 256, :]
        below = 1.0 + jnp.exp(-gate)
        sigmoid, silu = 1.0 / below, gate / below
        act_ref[t : t + 256, :] = (silu * up).astype(BF16)
        grad_gate = grad_act * up * sigmoid * (1.0 + gate * (1.0 - sigmoid))
        grads_ref[t : t + 256, :padded] = grad_gate.astype(BF16)
        grads_ref[t : t + 256, padded:] = (grad_act * silu).astype(BF16)


def outer_kernel(half, where_ref, mine_ref, other_ref, *refs):
    blocks, out_ref = refs[:-1], refs[-1]
    here = pl.ds(pl.multiple_of(where_ref[1] * half, 16), half)
    there = pl.ds(pl.multiple_of((1 - where_ref[1]) * half, 16), half)
    total = None
    for k, block in enumerate(blocks):
        part = dot_tn(mine_ref[k], block[here, :]) + dot_tn(other_ref[k], block[there, :])
        total = part if total is None else total + part
    out_ref[...] = total


def owned(got, other, where):
    far = len(got)
    _, count, half_hidden, slab = got[0].shape
    total = far * 4 * half_hidden
    return local_kernel(
        functools.partial(owned_kernel, far, count, half_hidden),
        [jax.ShapeDtypeStruct((slab, total), F32)] * count,
        [pltpu.VMEM((total, slab), F32)],
        where,
        *got,
        *other,
    )


def layer(
    plane,
    tokens_in,
    doc_positions,
    attn_gain,
    query_weight,
    key_weight,
    value_weight,
    output_weight,
    mlp_gain,
    gate_weight,
    up_weight,
    down_weight,
    cotangent,
):
    nf = plane.size
    me = lax.axis_index("fsdp")
    high, low = me // 2, me % 2
    ctx = lax.axis_index("ctx")
    core = lax.axis_index("tp")
    rows, width = tokens_in.shape
    half_rows = rows // 2
    slab = query_weight.shape[0]
    query_columns = query_weight.shape[1]
    key_columns = key_weight.shape[1]
    hidden = gate_weight.shape[1] // nf
    half_hidden = hidden // 2

    def my_half(array):
        return lax.dynamic_slice_in_dim(array, core * half_rows, half_rows, 0)

    def tp_order(mine, other):
        here = core == 0
        return jnp.where(here, mine, other), jnp.where(here, other, mine)

    def tp_sum(partial):
        return partial + plane.swap_tp(partial)

    def plane_rows(array):
        mine = jnp.concatenate(plane.gather(my_half(array)), axis=0)
        return mine, plane.swap_tp(mine)

    def columns_near(array):
        mine, parity = lax.optimization_barrier((my_half(array), low))
        blocks = [mine[:, i * slab : (i + 1) * slab] for i in range(nf)]
        return plane.exchange_near(blocks, parity)

    fences = Fences(doc_positions[0])

    gain_rows = jnp.zeros((16, query_columns + 2 * key_columns), BF16)
    gain_rows = gain_rows.at[0, :slab].set(attn_gain).at[1, :slab].set(mlp_gain)
    qkv_shard = jnp.concatenate(
        [jnp.concatenate([query_weight, key_weight, value_weight], axis=1), gain_rows], axis=0
    )
    shared_rows = slab * 5 // 16 // 16 * 16
    qkv_own, qkv_blocks, qkv_groups, qkv_others = plane.gather_shared(qkv_shard, ctx, shared_rows)
    wo_own, wo_blocks, wo_groups, wo_others = plane.gather_shared(output_weight, ctx, shared_rows)
    cot_all = plane_rows(cotangent)

    mlp_shard = jnp.stack([gate_weight.T, up_weight.T, down_weight.T])
    mlp_halves = mlp_shard.reshape(3, nf, 2, half_hidden, slab)
    mlp_sent = jnp.where(ctx == 0, mlp_halves[:, :, 0], mlp_halves[:, :, 1])
    mlp_kept, mlp_got = plane.exchange_near([mlp_sent[:, i] for i in range(nf)], low)
    mlp_blocks = plane.exchange_far(mlp_kept, mlp_got, high)

    fences.cut()
    fences.cut()
    fences.cut()
    fences.cut()
    fences.cut()
    tokens = tokens_in.astype(F32)
    rms_one = lax.rsqrt(jnp.mean(tokens * tokens, axis=-1, keepdims=True) + EPSILON)
    scaled_one = tokens * rms_one
    where = jnp.stack([me, core, ctx]).astype(jnp.int32)
    cosine, sine = pair_tables(doc_positions)
    queries, kv_mine, normed_one, gains, qkv_whole = local_kernel(
        functools.partial(project_in_kernel, slab, qkv_others),
        [
            jax.ShapeDtypeStruct((rows, query_columns), BF16),
            jax.ShapeDtypeStruct((rows, 2 * key_columns), BF16),
            jax.ShapeDtypeStruct((rows, width), BF16),
            jax.ShapeDtypeStruct((16, width), F32),
            jax.ShapeDtypeStruct((nf,) + qkv_shard.shape, BF16),
        ],
        [],
        where,
        tokens_in,
        cosine,
        sine,
        qkv_own,
        *qkv_blocks,
        *qkv_groups,
    )
    gain_one, gain_two = gains[0:1], gains[1:2]

    def outer(got, blocks):
        mine = jnp.concatenate(got)
        return local_kernel(
            functools.partial(outer_kernel, half_rows),
            [jax.ShapeDtypeStruct((slab, blocks[0].shape[1]), F32)],
            [],
            where,
            mine,
            plane.swap_tp(mine),
            *blocks,
        )[0]

    kv_other = plane.swap_ctx(kv_mine)
    kv_mine, queries = fences.cut(kv_mine, queries)
    kv_all = jnp.concatenate([kv_mine, kv_other], axis=0)
    positions = doc_positions[None, :]
    attended_low, lse = local_kernel(
        attend_kernel,
        [
            jax.ShapeDtypeStruct((rows, query_columns), BF16),
            jax.ShapeDtypeStruct((query_columns // 128, 2, rows), F32),
        ],
        [
            pltpu.VMEM((key_columns // HEAD_DIM, 2 * rows, HEAD_DIM), BF16),
            pltpu.VMEM((key_columns // HEAD_DIM, HEAD_DIM, 2 * rows), BF16),
        ],
        where,
        positions,
        queries,
        kv_all,
    )
    attended_low = fences.cut(attended_low)
    fences.cut()
    branch, wo_whole = local_kernel(
        functools.partial(project_gathered_kernel, slab, wo_others),
        [
            jax.ShapeDtypeStruct((rows, width), F32),
            jax.ShapeDtypeStruct((nf,) + output_weight.shape, BF16),
        ],
        [],
        where,
        attended_low,
        wo_own,
        *wo_blocks,
        *wo_groups,
    )
    residual = tokens + tp_sum(branch)
    rms_two = lax.rsqrt(jnp.mean(residual * residual, axis=-1, keepdims=True) + EPSILON)
    scaled_two = residual * rms_two
    normed_two = (scaled_two * gain_two).astype(BF16)

    normed_all = plane_rows(normed_two)
    fences.cut()
    fences.cut()
    fences.cut()
    fences.cut()
    padded = -(-hidden // 128) * 128
    gate_up_t, down_t = local_kernel(
        functools.partial(hidden_kernel, hidden, slab),
        [
            jax.ShapeDtypeStruct((2 * padded, width), BF16),
            jax.ShapeDtypeStruct((padded, width), BF16),
        ],
        [],
        where,
        *mlp_blocks,
        *(plane.swap_ctx(b) for b in mlp_blocks),
    )
    attended_all = plane.gather(attended_low)
    normed_near = columns_near(fences.after(normed_one))
    normed_got = plane.exchange_far(*normed_near, high)
    grads, acts = [], []
    for h in range(2):
        grad_h, act_h = local_kernel(
            feed_kernel,
            [
                jax.ShapeDtypeStruct((nf * half_rows, 2 * padded), BF16),
                jax.ShapeDtypeStruct((nf * half_rows, padded), BF16),
            ],
            [],
            where,
            normed_all[h],
            gate_up_t,
            dot_nt(cot_all[h], down_t),
        )
        grads.append(grad_h)
        acts.append(act_h)

    def ctx_half(whole, first):
        middle, last = first + half_hidden, first + hidden
        got = plane.swap_ctx(fences.after(whole[middle:last]))
        return sum(lax.optimization_barrier((whole[first:middle], got)))

    def owners_near(halves):
        blocks = [
            jnp.stack([h[:, i * slab : (i + 1) * slab] for h in halves]) for i in range(nf)
        ]
        return plane.exchange_near(blocks, low)

    def from_owners(got, where):
        other = [plane.swap_ctx(g) for g in got]
        return owned(got, other, where)

    def tp_part(lefts, right, wire):
        other = plane.swap_tp(dot_nn(lefts[1], right).astype(wire)).astype(F32)
        mine = dot_nn(lefts[0], right) + other
        return plane.reduce_near(mine.reshape(nf, half_rows, -1), wire)

    def whole_rows(mine):
        one, two = tp_order(mine, plane.swap_tp(mine))
        return jnp.concatenate([one, two], axis=0)

    pieces = 4
    step = width // pieces
    near = []
    reduced = []

    def piece(i):
        lefts = [fences.after(g) for g in grads]
        near.append(tp_part(lefts, gate_up_t[:, i * step : (i + 1) * step], F32))

    def piece_far(i):
        reduced.append(plane.reduce_far(near[i][0] + near[i][1]))

    grads[0], grads[1], acts[0], acts[1] = fences.cut(*grads, *acts)
    piece(0)
    piece(1)
    half_down = ctx_half(sum(dot_tn(fences.after(a), c) for a, c in zip(acts, cot_all)), 0)
    fences.cut()
    piece_far(0)
    piece(2)
    gate_up_grad = sum(dot_tn(fences.after(g), n) for g, n in zip(grads, normed_all))
    half_gate = ctx_half(gate_up_grad, 0)
    fences.cut()
    piece_far(1)
    piece(3)
    half_up = ctx_half(gate_up_grad, padded)
    fences.cut()
    piece_far(2)
    mlp_kept, mlp_odd = tp_part([fences.after(a) for a in acts], down_t, BF16)
    down_near = owners_near([half_down])
    fences.cut()
    piece_far(3)
    gate_up_near = owners_near([half_gate, half_up])
    fences.cut()
    down_got = plane.exchange_far(*down_near, high)
    fences.cut()
    grad_normed_two = whole_rows(jnp.concatenate(reduced, axis=-1))
    fences.cut()
    grad_out = cotangent.astype(F32)
    scaled_grad_two = grad_normed_two * gain_two
    grad_residual = (
        grad_out
        + rms_two * scaled_grad_two
        - residual
        * (rms_two * rms_two * rms_two)
        * jnp.mean(scaled_grad_two * residual, axis=-1, keepdims=True)
    )
    grad_attn_low = grad_residual.astype(BF16)
    grad_attended = local_kernel(
        functools.partial(project_back_kernel, slab),
        [jax.ShapeDtypeStruct((rows, query_columns), BF16)],
        [],
        where,
        grad_attn_low,
        wo_whole,
    )[0]
    grad_attn_near = columns_near(fences.after(grad_attn_low))
    grad_attended = fences.cut(grad_attended)
    grad_query, kv_grads = local_kernel(
        attend_back_kernel,
        [
            jax.ShapeDtypeStruct((rows, query_columns), BF16),
            jax.ShapeDtypeStruct((2 * rows, 2 * key_columns), F32),
        ],
        [],
        where,
        positions,
        queries,
        kv_all,
        lse,
        grad_attended,
        cosine,
        sine,
    )
    kv_grads, grad_query = fences.cut(kv_grads, grad_query)
    mlp_mine = plane.reduce_far(mlp_kept + mlp_odd.astype(F32), BF16)
    grad_attn_got = plane.exchange_far(*grad_attn_near, high)
    (grad_qkv_lin,) = local_kernel(
        finish_kv_kernel,
        [jax.ShapeDtypeStruct((rows, query_columns + 2 * key_columns), BF16)],
        [],
        where,
        grad_query,
        kv_grads[:rows],
        plane.swap_ctx(kv_grads[rows:]),
        cosine,
        sine,
    )
    grad_qkv_all = plane.gather(grad_qkv_lin)
    fences.cut()
    gate_up_got = plane.exchange_far(*gate_up_near, high)
    grad_normed_one = tp_sum(
        local_kernel(
            functools.partial(project_out_kernel, slab),
            [jax.ShapeDtypeStruct((rows, width), F32)],
            [],
            where,
            fences.after(grad_qkv_lin),
            qkv_whole,
        )[0],
    )
    fences.cut()
    gain_sums = plane.sum_all(
        jnp.stack(
            [
                jnp.sum(grad_normed_one * scaled_one, axis=0),
                jnp.sum(grad_normed_two * scaled_two, axis=0),
            ]
        ),
    )
    fences.cut()
    grad_wo = outer(grad_attn_got, [fences.after(b) for b in attended_all])
    fences.cut()
    grad_qkv = outer(normed_got, [fences.after(b) for b in grad_qkv_all])
    fences.cut()
    scaled_grad_one = grad_normed_one * gain_one
    grad_tokens = (
        grad_residual
        + rms_one * scaled_grad_one
        - tokens
        * (rms_one * rms_one * rms_one)
        * jnp.mean(scaled_grad_one * tokens, axis=-1, keepdims=True)
    )
    output_grad = grad_wo + plane.swap_ctx(grad_wo)
    (down_grad,) = from_owners(down_got, where)
    grad_tokens, output_grad, down_grad = fences.cut(grad_tokens, output_grad, down_grad)
    fences.cut()
    block_out = (fences.after(residual) + whole_rows(mlp_mine)).astype(BF16)
    grad_qkv = grad_qkv + plane.swap_ctx(grad_qkv)
    block_out, grad_qkv, last = lax.optimization_barrier((block_out, grad_qkv, where))
    query_grad = grad_qkv[:, :query_columns]
    key_grad = grad_qkv[:, query_columns : query_columns + key_columns]
    value_grad = grad_qkv[:, query_columns + key_columns :]
    gate_grad, up_grad = from_owners(gate_up_got, last)

    gain_sums = lax.dynamic_slice_in_dim(gain_sums, me * slab, slab, 1)
    gain_sums = jnp.where(fences.value > 0, gain_sums, 0.0)
    return (
        block_out,
        grad_tokens,
        gain_sums[0],
        query_grad,
        key_grad,
        value_grad,
        output_grad,
        gain_sums[1],
        gate_grad,
        up_grad,
        down_grad,
    )


def rotary_tables(positions):
    half_dim = HEAD_DIM // 2
    inverse = 1.0 / 10000.0 ** (jnp.arange(half_dim, dtype=F32) * (2.0 / HEAD_DIM))
    angles = positions.astype(F32)[:, None] * inverse[None, :]
    cosine_table = jnp.concatenate([jnp.cos(angles), jnp.cos(angles)], axis=-1)[:, None, :]
    sine_table = jnp.concatenate([jnp.sin(angles), jnp.sin(angles)], axis=-1)[:, None, :]
    return (cosine_table, sine_table)


def apply_rotary(values, cosine_table, sine_table):
    half_dim = values.shape[-1] // 2
    turned = jnp.concatenate([-values[..., half_dim:], values[..., :half_dim]], axis=-1)
    return values * cosine_table + turned * sine_table


def undo_rotary(gradient, cosine_table, sine_table):
    half_dim = gradient.shape[-1] // 2
    sined = gradient * sine_table
    return gradient * cosine_table + jnp.concatenate(
        [sined[..., half_dim:], -sined[..., :half_dim]], axis=-1
    )


def contract_last(left_array, right_array):
    return lax.dot_general(
        left_array, right_array, (((1,), (1,)), ((), ())), preferred_element_type=F32
    )


def contract_first(left_array, right_array):
    return lax.dot_general(
        left_array, right_array, (((0,), (0,)), ((), ())), preferred_element_type=F32
    )


def normed_fold(scaled, pieces):
    gain_float = pieces[0].astype(F32)
    normed = (scaled * gain_float[None, :]).astype(BF16)
    sums = tuple(
        (jnp.dot(normed, matrix, preferred_element_type=F32) for matrix in pieces[1:])
    )
    return sums + (normed, gain_float)


def row_fold(left_array, shard_piece):
    return jnp.dot(left_array, shard_piece, preferred_element_type=F32)


def column_fold(gradients_in, pieces):
    part_sum = contract_last(gradients_in[0], pieces[0])
    for grad_piece, weight_piece in zip(gradients_in[1:], pieces[1:]):
        part_sum = part_sum + contract_last(grad_piece, weight_piece)
    return part_sum


def column_map(left_array, shard_piece):
    return contract_last(left_array, shard_piece)


def tensor_total(partial_sum):
    return lax.psum(partial_sum, "tp")


def rows_body(
    tokens_in,
    doc_positions,
    attn_gain,
    query_weight,
    key_weight,
    value_weight,
    output_weight,
    mlp_gain,
    gate_weight,
    up_weight,
    down_weight,
    cotangent,
):
    local_rows = tokens_in.shape[0]
    query_columns = query_weight.shape[1]
    key_columns = key_weight.shape[1]
    local_groups = key_columns // HEAD_DIM
    group_size = HEADS // KV_HEADS
    group_width = group_size * HEAD_DIM
    score_scale = HEAD_DIM ** (-0.5)
    tokens = tokens_in.astype(F32)
    rms_one = lax.rsqrt(jnp.mean(tokens * tokens, axis=-1, keepdims=True) + EPSILON)
    scaled_one = tokens * rms_one
    query_lin, key_lin, value_lin, normed_one, gain_one = normed_fold(
        scaled_one,
        (
            lax.all_gather(attn_gain, "fsdp", axis=0, tiled=True),
            lax.all_gather(query_weight, "fsdp", axis=0, tiled=True),
            lax.all_gather(key_weight, "fsdp", axis=0, tiled=True),
            lax.all_gather(value_weight, "fsdp", axis=0, tiled=True),
        ),
    )
    cosine_table, sine_table = rotary_tables(doc_positions)
    queries = (
        apply_rotary(query_lin.reshape(local_rows, -1, HEAD_DIM), cosine_table, sine_table)
        .astype(BF16)
        .reshape(local_rows, query_columns)
    )
    keys_low = (
        apply_rotary(key_lin.reshape(local_rows, -1, HEAD_DIM), cosine_table, sine_table)
        .astype(BF16)
        .reshape(local_rows, key_columns)
    )
    values_low = value_lin.astype(BF16)
    key_all, value_all = (
        lax.all_gather(keys_low, "ctx", axis=0, tiled=True),
        lax.all_gather(values_low, "ctx", axis=0, tiled=True),
    )
    key_count = key_all.shape[0]
    query_places = lax.axis_index("ctx") * local_rows + jnp.arange(local_rows, dtype=jnp.int32)
    key_places = jnp.arange(key_count, dtype=jnp.int32)
    allowed = (key_places[None, :] <= query_places[:, None]) & (
        key_places[None, :] >= (query_places - doc_positions)[:, None]
    )

    def head_scores(query_group, key_head):
        raw_scores = (
            jnp.einsum("ngd,kd->gnk", query_group, key_head, preferred_element_type=F32)
            * score_scale
        )
        return jnp.where(allowed[None], raw_scores, NEG_FILL)

    attended_parts = []
    lse_parts = []
    for group_index in range(local_groups):
        query_group = queries[
            :, group_index * group_width : (group_index + 1) * group_width
        ].reshape(local_rows, group_size, HEAD_DIM)
        key_head = key_all[:, group_index * HEAD_DIM : (group_index + 1) * HEAD_DIM]
        value_head = value_all[:, group_index * HEAD_DIM : (group_index + 1) * HEAD_DIM]
        scores = head_scores(query_group, key_head)
        largest = jnp.max(scores, axis=-1, keepdims=True)
        exponent = jnp.exp(scores - largest)
        totals = jnp.sum(exponent, axis=-1, keepdims=True)
        probs_low = (exponent / totals).astype(BF16)
        attended_parts.append(
            jnp.einsum(
                "gnk,kd->ngd", probs_low, value_head, preferred_element_type=F32
            ).reshape(local_rows, group_width)
        )
        lse_parts.append(largest + jnp.log(totals))
    attended_low = jnp.concatenate(attended_parts, axis=1).astype(BF16)
    attn_branch = tensor_total(
        column_map(attended_low, lax.all_gather(output_weight, "fsdp", axis=0, tiled=True))
    )
    residual = tokens + attn_branch
    rms_two = lax.rsqrt(jnp.mean(residual * residual, axis=-1, keepdims=True) + EPSILON)
    scaled_two = residual * rms_two
    gate_lin, up_lin, normed_two, gain_two = normed_fold(
        scaled_two,
        (
            lax.all_gather(mlp_gain, "fsdp", axis=0, tiled=True),
            lax.all_gather(gate_weight, "fsdp", axis=0, tiled=True),
            lax.all_gather(up_weight, "fsdp", axis=0, tiled=True),
        ),
    )
    silu_value = gate_lin / (1.0 + jnp.exp(-gate_lin))
    act_low = (silu_value * up_lin).astype(BF16)
    mlp_branch = tensor_total(
        column_map(act_low, lax.all_gather(down_weight, "fsdp", axis=0, tiled=True))
    )
    block_out = (residual + mlp_branch).astype(BF16)
    grad_out = cotangent.astype(F32)
    grad_act = row_fold(cotangent, lax.all_gather(down_weight, "fsdp", axis=0, tiled=True))
    sigmoid = 1.0 / (1.0 + jnp.exp(-gate_lin))
    grad_gate_lin = (grad_act * up_lin * sigmoid * (1.0 + gate_lin * (1.0 - sigmoid))).astype(
        BF16
    )
    grad_up_lin = (grad_act * silu_value).astype(BF16)
    grad_normed_two = tensor_total(
        column_fold(
            (grad_gate_lin, grad_up_lin),
            (
                lax.all_gather(gate_weight, "fsdp", axis=0, tiled=True),
                lax.all_gather(up_weight, "fsdp", axis=0, tiled=True),
            ),
        )
    )
    scaled_grad_two = grad_normed_two * gain_two[None, :]
    grad_residual = (
        grad_out
        + rms_two * scaled_grad_two
        - residual
        * (rms_two * rms_two * rms_two)
        * jnp.mean(scaled_grad_two * residual, axis=-1, keepdims=True)
    )
    grad_attn_low = grad_residual.astype(BF16)
    grad_attended = row_fold(
        grad_attn_low, lax.all_gather(output_weight, "fsdp", axis=0, tiled=True)
    ).astype(BF16)
    query_grads = []
    key_grads = []
    value_grads = []
    for group_index in range(local_groups):
        query_group = queries[
            :, group_index * group_width : (group_index + 1) * group_width
        ].reshape(local_rows, group_size, HEAD_DIM)
        key_head = key_all[:, group_index * HEAD_DIM : (group_index + 1) * HEAD_DIM]
        value_head = value_all[:, group_index * HEAD_DIM : (group_index + 1) * HEAD_DIM]
        probabilities = jnp.exp(head_scores(query_group, key_head) - lse_parts[group_index])
        probs_low = probabilities.astype(BF16)
        grad_group = grad_attended[
            :, group_index * group_width : (group_index + 1) * group_width
        ].reshape(local_rows, group_size, HEAD_DIM)
        grad_probs = jnp.einsum(
            "ngd,kd->gnk", grad_group, value_head, preferred_element_type=F32
        )
        row_dot = jnp.sum(probabilities * grad_probs, axis=-1, keepdims=True)
        grad_scores = (probabilities * (grad_probs - row_dot)).astype(BF16)
        query_grads.append(
            jnp.einsum("gnk,kd->ngd", grad_scores, key_head, preferred_element_type=F32)
            * score_scale
        )
        key_grads.append(
            jnp.einsum("gnk,ngd->kd", grad_scores, query_group, preferred_element_type=F32)
            * score_scale
        )
        value_grads.append(
            jnp.einsum("gnk,ngd->kd", probs_low, grad_group, preferred_element_type=F32)
        )
    key_grad_local, value_grad_local = (
        lax.psum_scatter(
            jnp.concatenate(key_grads, axis=1), "ctx", scatter_dimension=0, tiled=True
        ),
        lax.psum_scatter(
            jnp.concatenate(value_grads, axis=1), "ctx", scatter_dimension=0, tiled=True
        ),
    )
    grad_q_lin = (
        undo_rotary(jnp.concatenate(query_grads, axis=1), cosine_table, sine_table)
        .astype(BF16)
        .reshape(local_rows, query_columns)
    )
    grad_k_lin = (
        undo_rotary(key_grad_local.reshape(local_rows, -1, HEAD_DIM), cosine_table, sine_table)
        .astype(BF16)
        .reshape(local_rows, key_columns)
    )
    grad_v_lin = value_grad_local.astype(BF16)
    grad_normed_one = tensor_total(
        column_fold(
            (grad_q_lin, grad_k_lin, grad_v_lin),
            (
                lax.all_gather(query_weight, "fsdp", axis=0, tiled=True),
                lax.all_gather(key_weight, "fsdp", axis=0, tiled=True),
                lax.all_gather(value_weight, "fsdp", axis=0, tiled=True),
            ),
        )
    )
    scaled_grad_one = grad_normed_one * gain_one[None, :]
    grad_tokens = (
        grad_residual
        + rms_one * scaled_grad_one
        - tokens
        * (rms_one * rms_one * rms_one)
        * jnp.mean(scaled_grad_one * tokens, axis=-1, keepdims=True)
    )
    owned = lax.psum_scatter(
        (
            jnp.sum(grad_normed_one * scaled_one, axis=0),
            contract_first(normed_one, grad_q_lin),
            contract_first(normed_one, grad_k_lin),
            contract_first(normed_one, grad_v_lin),
            contract_first(grad_attn_low, attended_low),
            jnp.sum(grad_normed_two * scaled_two, axis=0),
            contract_first(normed_two, grad_gate_lin),
            contract_first(normed_two, grad_up_lin),
            contract_first(cotangent, act_low),
        ),
        "fsdp",
        scatter_dimension=0,
        tiled=True,
    )
    (
        gain_one_grad,
        query_grad,
        key_grad,
        value_grad,
        output_grad,
        gain_two_grad,
        gate_grad,
        up_grad,
        down_grad,
    ) = owned
    summed = lax.psum(
        (
            gain_one_grad,
            query_grad,
            key_grad,
            value_grad,
            output_grad,
            gain_two_grad,
            gate_grad,
            up_grad,
            down_grad,
        ),
        "ctx",
    )
    return (
        block_out,
        grad_tokens,
        summed[0],
        summed[1],
        summed[2],
        summed[3],
        summed[4],
        summed[5],
        summed[6],
        summed[7],
        summed[8],
    )


def choose_body(size, *arrays):
    rows, width = arrays[0].shape
    if size * rows <= width:
        return layer(Plane(size), *arrays)
    return rows_body(*arrays)


def solution(mesh):
    rows = P(("fsdp", "ctx"), None)
    weight = P("fsdp", "tp")
    gain = P("fsdp")
    return jax.shard_map(
        functools.partial(choose_body, mesh.shape["fsdp"]),
        mesh=mesh,
        in_specs=(
            rows,
            P(("fsdp", "ctx")),
            gain,
            weight,
            weight,
            weight,
            weight,
            gain,
            weight,
            weight,
            weight,
            rows,
        ),
        out_specs=(rows, rows, gain, weight, weight, weight, weight, gain, weight, weight, weight),
        check_vma=False,
    )
```
